512 devices in a mesh: batch: 64 (over z, y_hi, core), coef: 8 (over y_lo, x).
Axes of the slice: x: 4, y: 4 (y_hi: 2, y_lo: 2; y = y_hi * 2 + y_lo), z: 16, core: 2. Of those that a mesh axis runs over, the one named last changes fastest.
Arguments:
- jac_blocks: bfloat16 [2048, 8, 2, 128, 128], P(('batch', 'coef')), may hold values from -0.52734375 to 0.52734375
- col_blocks: int32 [8, 2048, 2], P('coef', 'batch'), may hold values from 0 to 63, all different within a row; in each aligned block of 32 rows (0 to 31, 32 to 63, ..., all dimensions but the last counted through in order) at most 2 rows name the same one
- residual: float32 [2048, 128], P('batch'), may hold values from -6 to 6
- run_of_half: int32 [4096], P('batch'), may hold values from 0 to 4095, each once
- run_scale: bfloat16 [4096], replicated, may hold values from 0.25 to 4
Outputs:
- diag_blocks: float32 [8, 64, 128, 128], P('coef', 'batch')
- gradient: float32 [8, 64, 128], P('coef', 'batch')
The draws below stay inside these ranges and needn't reach their ends.
Inputs may be any that keep to these rules, and one draw needn't show every extreme that they name: `col_blocks`: the 2 column blocks of one row block in one group differ. For each group, among the row blocks of one batch index (aligned blocks of the row-block dimension), no column block is named more than 2 times, a bound that some block reaches. `run_of_half`: every run appears exactly once.
All inputs are finite; a program needn't handle non-finite values.
Results may differ from the reference program's by a relative error of at most 0.00043.
Values may be sent and summed in bfloat16 or wider, within the bound.
No kernel may reach another device: no remote copies, remote signals or barrier semaphores. Data moves between devices by JAX's collectives and lax.ppermute only.
A program may use at most 64 MiB of HBM per device.

```python
import math
import jax
import jax.numpy as jnp
import numpy as np
from jax import lax

BS = 128
PAIR = 2
CAP = 2
R_DEV = 4
G = 8
LCB = 64
NRB = 2048
RUNS = 4096
N_COEF = 8


def steps_of(own_key, dims, cuts, low, largest):
    factor_of, own = 1.0, jax.random.fold_in(own_key, 6)
    for position, blocks in cuts:
        steps = jnp.exp(jax.random.uniform(jax.random.fold_in(own, position), (blocks,), jnp.float32, low / len(cuts), largest / len(cuts)))
        factor_of = factor_of * jnp.repeat(steps, dims[position] // blocks).reshape([-1 if axis == position else 1 for axis in range(len(dims))])
    return factor_of


def assign_block(key, own, number, rows, count, top, limit, slope):
    order = jax.random.permutation(key, count)
    packed, common = portions_of(count, rows * top, limit, slope, True), portions_of(count, rows * top, limit, slope, False)
    places = jnp.arange(count)

    def named(tallies, offset_by):
        used = int((tallies > 0).sum())
        fixed = max(1, used // 4)
        moved = fixed + (places - fixed + offset_by * (used - fixed)) % max(1, count - fixed)
        return jnp.zeros((count,), jnp.int32).at[order[jnp.where(places < fixed, places, moved)]].set(jnp.asarray(tallies, jnp.int32))

    tallies = jnp.where(number % 4 == 0, named(packed, number // 4), named(common, number - number // 4 - 1))
    mixed = jax.random.permutation(jax.random.fold_in(own, 3), count)
    donor, receiver = mixed[0:count // 2 * 2:2], mixed[1:count // 2 * 2:2]
    margin = jnp.minimum(tallies[donor] - 1, limit - tallies[receiver]) // 2
    margin = jnp.where((donor == order[0]) | (receiver == order[0]) | (tallies[receiver] == 0), 0, jnp.maximum(margin, 0))
    moved = jax.random.randint(jax.random.fold_in(own, 4), (count // 2,), 0, 1 << 20) % (margin + 1)
    tallies = tallies.at[donor].add(-moved).at[receiver].add(moved)
    members = jnp.searchsorted(jnp.cumsum(tallies), jnp.arange(rows * top), side="right").astype(jnp.int32)
    table = members.reshape(top, rows).T
    table = table[jax.random.permutation(jax.random.fold_in(own, 1), rows)]
    offset_by = jax.random.randint(jax.random.fold_in(own, 2), (rows, 1), 0, top)
    return jnp.take_along_axis(table, (jnp.arange(top)[None, :] + offset_by) % top, axis=1)


def portions_of(number_of, total, bound, skew, full):
    loads = [(1 << 20) // math.isqrt(standing ** skew) + 1 for standing in range(1, number_of + 1)]
    largest = bound if full else min(bound, max(-(-total // number_of), total * loads[0] // sum(loads)))
    least = 1 if total - largest >= number_of - 1 else 0
    given, rest = [largest] + [least] * (number_of - 1), total - largest - least * (number_of - 1)
    while rest > 0:
        movable = [i for i in range(1, number_of) if given[i] < largest] or [i for i in range(1, number_of) if given[i] < bound]
        mass, left = sum([loads[i] for i in movable]), rest
        for i in movable:
            more = min(bound - given[i], max(1, left * loads[i] // mass), rest)
            given[i] = given[i] + more
            rest = rest - more
    return np.array(given)


def noise(own_key, shape, width, reach, cuts=(), kind=jnp.bfloat16):
    result = jax.random.normal(own_key, shape, jnp.float32) * width
    if len(cuts) > 0:
        result = steps_of(own_key, shape, cuts, -0.22, 0.18) * result
    return jnp.clip(result, min=-reach, max=reach).astype(kind)


def setup_inputs(seed: int = 0) -> dict:
    splits = jax.random.split(jax.random.key(seed), 6)
    jac_blocks = noise(splits[0], (NRB, G, PAIR, BS, BS), (1.0 / BS ** 0.5), 0.52734375, ((0, 512),))
    col_blocks_keys = jax.random.split(jax.random.fold_in(splits[1], 1), G * NRB // (R_DEV * N_COEF))
    col_blocks_turns = jax.random.permutation(jax.random.fold_in(splits[1], 3), G * NRB // (R_DEV * N_COEF))
    col_blocks = jax.vmap(lambda own, number: assign_block(jax.random.fold_in(splits[1], 2), own, number, R_DEV * N_COEF, LCB, PAIR, CAP, 2))(col_blocks_keys, col_blocks_turns).reshape((G, NRB, PAIR))
    residual = noise(splits[2], (NRB, BS), 1.0, 6.0, ((0, 64),), jnp.float32)
    run_of_half = jax.random.permutation(splits[3], RUNS).astype(jnp.int32)
    run_scale = jnp.clip(jnp.exp(jax.random.uniform(splits[4], (RUNS,), jnp.float32, math.log(0.25), math.log(4.0))), 0.25, 4.0).astype(jnp.bfloat16)
    return dict(jac_blocks=jac_blocks, col_blocks=col_blocks, residual=residual, run_of_half=run_of_half, run_scale=run_scale)


def reference(jac_blocks, col_blocks, residual, run_of_half, run_scale):
    scale_rows = run_scale.astype(jnp.float32)[run_of_half].reshape(NRB, 2)
    weights = jnp.repeat(scale_rows, BS // 2, axis=1)
    cols_by_row = jnp.transpose(col_blocks, (1, 0, 2)).astype(jnp.int32)
    group_index = jnp.broadcast_to(jnp.arange(G, dtype=jnp.int32)[:, None], (G, PAIR))

    def step(carry, inputs):
        diag, grad = carry
        blocks, cols, res, wrow = inputs
        wide = blocks.astype(jnp.float32)
        rounded = (wide * wrow[None, None, :, None]).astype(jnp.bfloat16)
        weighted = lax.optimization_barrier(rounded).astype(jnp.float32)
        prod = jnp.einsum('gsak,gsab->gskb', wide, weighted, precision=lax.Precision.HIGHEST)
        gterm = jnp.einsum('gsak,a->gsk', wide, wrow * res, precision=lax.Precision.HIGHEST)
        diag = diag.at[group_index, cols].add(prod)
        grad = grad.at[group_index, cols].add(gterm)
        return (diag, grad), None

    init = (jnp.zeros((G, LCB, BS, BS), jnp.float32), jnp.zeros((G, LCB, BS), jnp.float32))
    (diag, grad), unused = lax.scan(step, init, (jac_blocks, cols_by_row, residual.astype(jnp.float32), weights))
    return diag, grad
```

```python
import functools

import jax
import jax.numpy as jnp
from jax import lax
from jax.experimental import pallas as pl
from jax.experimental.pallas import tpu as pltpu
from jax.sharding import Mesh
from jax.sharding import PartitionSpec as P

BS = 128
HALF = BS // 2
PAIR = 2
ROWS = HALF + 8
CODED = HALF + 16
FULL = 32000.0
STEPS = 16.0
TINY = 1e-30
VMEM = 48 * 1024 * 1024


def iota(shape, dim):
    return lax.broadcasted_iota(jnp.int32, shape, dim)


def products_kernel(unroll, targets, core, items, weights, residual, own, other, acc):
    n_items = items.shape[0]
    acc[...] = jnp.zeros_like(acc)
    upper = iota((HALF, BS), 1) >= iota((HALF, BS), 0)
    lanes = iota((HALF, BS), 1) == iota((HALF, BS), 0)
    sub = iota((8, BS), 0)

    def step(block, carry):
        for j in range(unroll):
            row = block * unroll + j
            w = weights[pl.ds(row, 1), :]
            wr = w * residual[pl.ds(row, 1), :]
            hi = wr.astype(jnp.bfloat16).astype(jnp.float32)
            mid = (wr - hi).astype(jnp.bfloat16).astype(jnp.float32)
            low = wr - hi - mid
            terms = jnp.where(sub == 0, hi, jnp.where(sub == 1, mid, jnp.where(sub == 2, low, 0.0)))
            terms = jnp.concatenate([terms, jnp.zeros_like(terms)], axis=0).astype(jnp.bfloat16)
            for s in range(PAIR):
                item = row * PAIR + s
                jac = items[item]
                scaled = (jac.T.astype(jnp.float32) * w).astype(jnp.bfloat16)
                left = jnp.concatenate([scaled, terms], axis=0)
                out = lax.dot_general(left, jac, (((1,), (0,)), ((), ())), preferred_element_type=jnp.float32)
                last = pltpu.roll(out[HALF:BS], HALF, 1)
                packed = jnp.where(upper, out[:HALF], last)
                diag = jnp.sum(jnp.where(lanes, last, 0.0), axis=0, keepdims=True)
                grad = jnp.sum(out[BS : BS + 8], axis=0, keepdims=True)
                tail = jnp.where(sub == 0, diag, jnp.where(sub == 1, grad, 0.0))
                where = targets[item]
                acc[where, :HALF] += packed
                acc[where, HALF:] += tail
        return carry

    lax.fori_loop(0, n_items // (PAIR * unroll), step, 0)
    me = core[0]

    def split(i, carry):
        own[i] = acc[2 * i + me]
        other[i] = acc[2 * i + 1 - me]
        return carry

    lax.fori_loop(0, own.shape[0], split, 0, unroll=4)


def encode_slot(value, coded, i):
    sub = iota((16, BS), 0)
    packed, tail = value[:HALF], value[HALF:]
    diag, grad = tail[0:1], tail[1:2]
    big = jnp.maximum(jnp.max(jnp.abs(packed), axis=0, keepdims=True), jnp.maximum(jnp.abs(diag), TINY))
    big_g = jnp.maximum(jnp.abs(grad), TINY)
    per = STEPS / 0.6931471805599453
    code = jnp.ceil(jnp.log(big) * per)
    code_g = jnp.ceil(jnp.log(big_g) * per)
    inv = jnp.exp2(code * (-1.0 / STEPS)) * FULL
    inv_g = jnp.exp2(code_g * (-1.0 / STEPS)) * FULL
    coded[i, :HALF] = jnp.round(packed * inv).astype(jnp.int32).astype(jnp.int16)
    g = grad * inv_g
    g_hi = jnp.round(g)
    g_lo = jnp.round((g - g_hi) * FULL)
    rows = [jnp.round(diag * inv), code, code_g, g_hi, g_lo]
    out = jnp.zeros((16, BS), jnp.float32)
    for k, row in enumerate(rows):
        out = jnp.where(sub == k, row, out)
    coded[i, HALF:] = out.astype(jnp.int32).astype(jnp.int16)


def add_kernel(unroll, own, got, coded):
    def step(block, carry):
        for j in range(unroll):
            i = block * unroll + j
            encode_slot(own[i] + got[i], coded, i)
        return carry

    lax.fori_loop(0, coded.shape[0] // unroll, step, 0)


def finish_kernel(coded, diag_out, grad_out):
    packed = jnp.zeros((HALF, BS), jnp.float32)
    diag = jnp.zeros((1, BS), jnp.float32)
    grad = jnp.zeros((1, BS), jnp.float32)
    for i in range(coded.shape[0]):
        tail = coded[i, HALF:].astype(jnp.int32).astype(jnp.float32)
        scale = jnp.exp2(tail[1:2] * (1.0 / STEPS)) * (1.0 / FULL)
        scale_g = jnp.exp2(tail[2:3] * (1.0 / STEPS)) * (1.0 / FULL)
        packed = packed + coded[i, :HALF].astype(jnp.int32).astype(jnp.float32) * scale
        diag = diag + tail[0:1] * scale
        grad = grad + (tail[3:4] + tail[4:5] * (1.0 / FULL)) * scale_g
    whole = jnp.concatenate([packed, pltpu.roll(packed, HALF, 1)], axis=0)
    flipped = whole.T
    r, c = iota((BS, BS), 0), iota((BS, BS), 1)
    plain = ((r < HALF) & (c >= r)) | ((c >= HALF) & (c < r))
    on = (r == c) & (r >= HALF)
    diag_out[...] = jnp.where(on, pltpu.roll(diag, HALF, 1), jnp.where(plain, whole, flipped))
    grad_out[...] = grad


def call(body, outs, scratch=(), smem=0, n_in=1, flops=0, moved=0):
    spec = pl.BlockSpec(memory_space=pltpu.VMEM)
    many = isinstance(outs, (list, tuple))
    return pl.pallas_call(
        body,
        out_shape=outs,
        in_specs=[pl.BlockSpec(memory_space=pltpu.SMEM)] * smem + [spec] * n_in,
        out_specs=[spec] * len(outs) if many else spec,
        scratch_shapes=list(scratch),
        compiler_params=pltpu.CompilerParams(vmem_limit_bytes=VMEM),
        cost_estimate=pl.CostEstimate(flops=flops, bytes_accessed=moved, transcendentals=0),
    )


def shards(jac_blocks, col_blocks, residual, run_of_half, run_scale):
    slots = lax.axis_size("z") * 4
    f32 = jnp.float32
    moved = lax.all_to_all(jac_blocks, "coef", split_axis=1, concat_axis=0, tiled=True)
    items = moved.reshape(-1, BS, BS)
    n_items = items.shape[0]
    targets = col_blocks.reshape(-1)
    scale_rows = run_scale.astype(f32)[run_of_half].reshape(-1, 2)
    weights = jnp.repeat(scale_rows, HALF, axis=1)
    me = lax.axis_index("core").astype(jnp.int32).reshape(1)
    piece = jax.ShapeDtypeStruct((slots // 2, ROWS, BS), f32)
    own, other = call(
        functools.partial(products_kernel, 2),
        [piece, piece],
        scratch=[pltpu.VMEM((slots, ROWS, BS), f32)],
        smem=2,
        n_in=3,
        flops=2 * n_items * BS**3,
        moved=n_items * BS * BS * 2 + slots * ROWS * BS * 4,
    )(targets, me, items, weights, residual)
    got = lax.ppermute(other, "core", [(0, 1), (1, 0)])
    coded = call(
        functools.partial(add_kernel, 4),
        jax.ShapeDtypeStruct((slots // 2, CODED, BS), jnp.int16),
        n_in=2,
        flops=slots * ROWS * BS * 8,
        moved=slots * ROWS * BS * 6,
    )(own, got)
    landed = lax.all_to_all(coded, ("z", "yh"), 0, 0, tiled=True)
    diag, grad = call(
        finish_kernel,
        [jax.ShapeDtypeStruct((BS, BS), f32), jax.ShapeDtypeStruct((1, BS), f32)],
        flops=slots * ROWS * BS * 4,
        moved=slots * ROWS * BS,
    )(landed)
    return diag.reshape(1, 1, BS, BS), grad.reshape(1, 1, BS)


def solution(mesh):
    fine = Mesh(mesh.devices.reshape(-1, 2, 2, mesh.devices.shape[1]), ("z", "yh", "core", "coef"))
    batch = ("z", "yh", "core")
    in_specs = (
        P(batch + ("coef",), None, None, None, None),
        P("coef", batch, None),
        P(batch, None),
        P(batch),
        P(),
    )
    out_specs = (P("coef", batch, None, None), P("coef", batch, None))
    return jax.shard_map(shards, mesh=fine, in_specs=in_specs, out_specs=out_specs, check_vma=False)
```

```python
import functools
import math

import jax
import jax.numpy as jnp
from jax import lax
from jax.experimental import pallas as pl
from jax.experimental.pallas import tpu as pltpu
from jax.sharding import Mesh
from jax.sharding import PartitionSpec as P

BS = 128
HALF = BS // 2
PAIR = 2
ROWS = HALF + 8
FULL = 32000.0
STEPS = 16.0
TINY = 1e-30
VMEM = 48 * 1024 * 1024
PER = STEPS / 0.6931471805599453


def iota(shape, dim):
    return lax.broadcasted_iota(jnp.int32, shape, dim)


def stack_rows(rows):
    sub = iota((8, BS), 0)
    out = jnp.zeros((8, BS), jnp.float32)
    for k, row in enumerate(rows):
        out = jnp.where(sub == k, row, out)
    return out


def to_int16(x):
    return jnp.round(x).astype(jnp.int32).astype(jnp.int16)


def loop(n, unroll, body):
    unroll = math.gcd(n, unroll)

    def step(block, carry):
        for j in range(unroll):
            body(block * unroll + j)
        return carry

    lax.fori_loop(0, n // unroll, step, 0)


def encode(packed, diag, grad):
    big = jnp.maximum(jnp.max(jnp.abs(packed), axis=0, keepdims=True), jnp.maximum(jnp.abs(diag), TINY))
    big_g = jnp.maximum(jnp.abs(grad), TINY)
    code = jnp.ceil(jnp.log(big) * PER)
    code_g = jnp.ceil(jnp.log(big_g) * PER)
    inv = jnp.exp2(code * (-1.0 / STEPS)) * FULL
    inv_g = jnp.exp2(code_g * (-1.0 / STEPS)) * FULL
    g = grad * inv_g
    g_hi = jnp.round(g)
    g_lo = (g - g_hi) * FULL
    return to_int16(packed * inv), to_int16(stack_rows([diag * inv, code, code_g, g_hi, g_lo]))


def decode(main, tail):
    tail = tail.astype(jnp.int32).astype(jnp.float32)
    scale = jnp.exp2(tail[1:2] * (1.0 / STEPS)) * (1.0 / FULL)
    scale_g = jnp.exp2(tail[2:3] * (1.0 / STEPS)) * (1.0 / FULL)
    packed = main.astype(jnp.int32).astype(jnp.float32) * scale
    return packed, tail[0:1] * scale, (tail[3:4] + tail[4:5] * (1.0 / FULL)) * scale_g


def products_kernel(unroll, place, weights, residual, jac_hbm, coded, jac, sem):
    n_rows, groups = jac_hbm.shape[:2]
    copies = [pltpu.make_async_copy(jac_hbm.at[r], jac.at[r], sem.at[r]) for r in range(n_rows)]
    for copy in copies:
        copy.start()
    upper = iota((HALF, BS), 1) >= iota((HALF, BS), 0)
    lanes = iota((HALF, BS), 1) == iota((HALF, BS), 0)
    for r in range(n_rows):
        w = weights[pl.ds(r, 1), :]
        wr = w * residual[pl.ds(place[0] * n_rows + r, 1), :]
        hi = wr.astype(jnp.bfloat16).astype(jnp.float32)
        mid = (wr - hi).astype(jnp.bfloat16).astype(jnp.float32)
        terms = stack_rows([hi, mid, wr - hi - mid])
        terms = jnp.concatenate([terms, jnp.zeros_like(terms)], axis=0).astype(jnp.bfloat16)
        copies[r].wait()

        def body(g):
            for s in range(PAIR):
                one = jac[r, g, s]
                scaled = (one.T.astype(jnp.float32) * w).astype(jnp.bfloat16)
                left = jnp.concatenate([scaled, terms], axis=0)
                out = lax.dot_general(left, one, (((1,), (0,)), ((), ())), preferred_element_type=jnp.float32)
                last = pltpu.roll(out[HALF:BS], HALF, 1)
                packed = jnp.where(upper, out[:HALF], last)
                diag = jnp.sum(jnp.where(lanes, last, 0.0), axis=0, keepdims=True)
                grad = jnp.sum(out[BS : BS + 8], axis=0, keepdims=True)
                main, tail = encode(packed, diag, grad)
                coded[g, r * PAIR + s, :HALF] = main
                coded[g, r * PAIR + s, HALF:] = tail

        loop(groups, unroll, body)


def place_kernel(unroll, targets, core, coded, own, other, acc):
    acc[...] = jnp.zeros_like(acc)

    def body(i):
        packed, diag, grad = decode(coded[i, :HALF], coded[i, HALF:])
        where = targets[i]
        acc[where, :HALF] += packed
        acc[where, HALF:] += stack_rows([diag, grad])

    loop(coded.shape[0], unroll, body)
    me = core[0]

    def split(i):
        own[i] = acc[2 * i + me]
        other[i] = acc[2 * i + 1 - me]

    loop(own.shape[0], unroll, split)


def halve_kernel(unroll, part, own, got, kept, coded):
    me = part[0]

    def body(i):
        mine, theirs = 2 * i + me, 2 * i + 1 - me
        kept[i] = own[mine] + got[mine]
        value = own[theirs] + got[theirs]
        coded[i, :HALF], coded[i, HALF:] = encode(value[:HALF], value[HALF : HALF + 1], value[HALF + 1 : HALF + 2])

    loop(coded.shape[0], unroll, body)


def recode_kernel(unroll, kept, got, coded):
    def body(i):
        packed, diag, grad = decode(got[i, :HALF], got[i, HALF:])
        tail = kept[i, HALF:]
        coded[i, :HALF], coded[i, HALF:] = encode(kept[i, :HALF] + packed, tail[0:1] + diag, tail[1:2] + grad)

    loop(coded.shape[0], unroll, body)


def finish_kernel(coded, diag_out, grad_out):
    packed = jnp.zeros((HALF, BS), jnp.float32)
    diag = jnp.zeros((1, BS), jnp.float32)
    grad = jnp.zeros((1, BS), jnp.float32)
    for i in range(coded.shape[0]):
        more = decode(coded[i, :HALF], coded[i, HALF:])
        packed, diag, grad = packed + more[0], diag + more[1], grad + more[2]
    whole = jnp.concatenate([packed, pltpu.roll(packed, HALF, 1)], axis=0)
    flipped = whole.T
    r, c = iota((BS, BS), 0), iota((BS, BS), 1)
    plain = ((r < HALF) & (c >= r)) | ((c >= HALF) & (c < r))
    on = (r == c) & (r >= HALF)
    diag_out[...] = jnp.where(on, pltpu.roll(diag, HALF, 1), jnp.where(plain, whole, flipped))
    grad_out[...] = grad


def call(body, outs, specs, scratch=(), flops=0, moved=0):
    spaces = {"v": pltpu.VMEM, "s": pltpu.SMEM, "a": pl.ANY}
    spec = pl.BlockSpec(memory_space=pltpu.VMEM)
    many = isinstance(outs, (list, tuple))
    return pl.pallas_call(
        body,
        out_shape=outs,
        in_specs=[pl.BlockSpec(memory_space=spaces[k]) for k in specs],
        out_specs=[spec] * len(outs) if many else spec,
        scratch_shapes=list(scratch),
        compiler_params=pltpu.CompilerParams(vmem_limit_bytes=VMEM),
        cost_estimate=pl.CostEstimate(flops=flops, bytes_accessed=moved, transcendentals=0),
    )


def shards(jac_blocks, col_blocks, residual, run_of_half, run_scale):
    f32, i16 = jnp.float32, jnp.int16
    slots = lax.axis_size("z") * 4
    n_rows, groups = jac_blocks.shape[:2]
    n_items = n_rows * groups * PAIR

    def index(name):
        return lax.axis_index(name).astype(jnp.int32).reshape(1)

    def shape(n, dtype):
        return jax.ShapeDtypeStruct((n, ROWS, BS), dtype)

    coef = index("coef")
    runs = lax.dynamic_slice_in_dim(run_of_half, coef[0] * n_rows * 2, n_rows * 2)
    weights = jnp.repeat(run_scale[runs].astype(f32).reshape(n_rows, 2), HALF, axis=1)
    coded = call(
        functools.partial(products_kernel, 2),
        jax.ShapeDtypeStruct((groups, n_rows * PAIR, ROWS, BS), i16),
        "svva",
        scratch=[pltpu.VMEM(jac_blocks.shape, jnp.bfloat16), pltpu.SemaphoreType.DMA((n_rows,))],
        flops=2 * n_items * BS**3,
        moved=n_items * BS * BS * 3,
    )(coef, weights, residual, jac_blocks)
    landed = lax.all_to_all(coded, "coef", 0, 0, tiled=True).reshape(n_items, ROWS, BS)
    own, other = call(
        functools.partial(place_kernel, 4),
        [shape(slots // 2, f32)] * 2,
        "ssv",
        scratch=[pltpu.VMEM((slots, ROWS, BS), f32)],
    )(col_blocks.reshape(-1), index("core"), landed)
    got = lax.ppermute(other, "core", [(0, 1), (1, 0)])
    kept, coded = call(
        functools.partial(halve_kernel, 4), [shape(slots // 4, f32), shape(slots // 4, i16)], "svv"
    )(index("yh"), own, got)
    got = lax.ppermute(coded, "yh", [(0, 1), (1, 0)])
    coded = call(functools.partial(recode_kernel, 4), shape(slots // 4, i16), "vv")(kept, got)
    landed = lax.all_to_all(coded, "z", 0, 0, tiled=True)
    diag, grad = call(
        finish_kernel, [jax.ShapeDtypeStruct((BS, BS), f32), jax.ShapeDtypeStruct((1, BS), f32)], "v"
    )(landed)
    return diag.reshape(1, 1, BS, BS), grad.reshape(1, 1, BS)


def solution(mesh):
    fine = Mesh(mesh.devices.reshape(-1, 2, 2, mesh.devices.shape[1]), ("z", "yh", "core", "coef"))
    batch = ("z", "yh", "core")
    in_specs = (
        P(batch + ("coef",), None, None, None, None),
        P("coef", batch, None),
        P(batch, None),
        P(batch),
        P(),
    )
    out_specs = (P("coef", batch, None, None), P("coef", batch, None))
    return jax.shard_map(shards, mesh=fine, in_specs=in_specs, out_specs=out_specs, check_vma=False)
```

```python
import functools
import math

import jax
import jax.numpy as jnp
from jax import lax
from jax.experimental import pallas as pl
from jax.experimental.pallas import tpu as pltpu
from jax.sharding import Mesh
from jax.sharding import PartitionSpec as P

BS = 128
HALF = BS // 2
PAIR = 2
ROWS = HALF + 8
FULL = 32000.0
STEPS = 16.0
TINY = 1e-30
PER = STEPS / 0.6931471805599453


def iota(shape, dim):
    return lax.broadcasted_iota(jnp.int32, shape, dim)


def stack_rows(rows):
    sub = iota((8, BS), 0)
    out = jnp.zeros((8, BS), jnp.float32)
    for k, row in enumerate(rows):
        out = jnp.where(sub == k, row, out)
    return out


def to_int16(x):
    return jnp.round(x).astype(jnp.int32).astype(jnp.int16)


def loop(n, unroll, body):
    unroll = math.gcd(n, unroll)

    def step(block, carry):
        for j in range(unroll):
            body(block * unroll + j)
        return carry

    lax.fori_loop(0, n // unroll, step, 0)


def encode(packed, diag, grad):
    big = jnp.maximum(jnp.max(jnp.abs(packed), axis=0, keepdims=True), jnp.maximum(jnp.abs(diag), TINY))
    big_g = jnp.maximum(jnp.abs(grad), TINY)
    code = jnp.ceil(jnp.log(big) * PER)
    code_g = jnp.ceil(jnp.log(big_g) * PER)
    inv = jnp.exp2(code * (-1.0 / STEPS)) * FULL
    inv_g = jnp.exp2(code_g * (-1.0 / STEPS)) * FULL
    g = grad * inv_g
    g_hi = jnp.round(g)
    g_lo = (g - g_hi) * FULL
    return to_int16(packed * inv), to_int16(stack_rows([diag * inv, code, code_g, g_hi, g_lo]))


def decode(main, tail):
    tail = tail.astype(jnp.int32).astype(jnp.float32)
    scale = jnp.exp2(tail[1:2] * (1.0 / STEPS)) * (1.0 / FULL)
    scale_g = jnp.exp2(tail[2:3] * (1.0 / STEPS)) * (1.0 / FULL)
    packed = main.astype(jnp.int32).astype(jnp.float32) * scale
    return packed, tail[0:1] * scale, (tail[3:4] + tail[4:5] * (1.0 / FULL)) * scale_g


def products_kernel(unroll, place, runs, scales_hbm, residual_hbm, jac_hbm, out_hbm, jac, coded, scales, residual, table, sem, out_sem, aux_sem):
    n_rows, groups = jac_hbm.shape[:2]
    copies = [pltpu.make_async_copy(jac_hbm.at[r], jac.at[r], sem.at[r]) for r in range(n_rows)]
    aux = [
        pltpu.make_async_copy(scales_hbm, scales, aux_sem.at[0]),
        pltpu.make_async_copy(residual_hbm, residual, aux_sem.at[1]),
    ]
    for copy in aux + copies:
        copy.start()
    done = []
    for copy in aux:
        copy.wait()
    table[...] = scales[...].astype(jnp.float32)
    upper = iota((HALF, BS), 1) >= iota((HALF, BS), 0)
    lanes = iota((HALF, BS), 1) == iota((HALF, BS), 0)
    lane = iota((1, BS), 1)

    def scale(half):
        run = runs[half]
        line = table[pl.ds(lax.div(run, BS), 1), :]
        return jnp.sum(jnp.where(lane == lax.rem(run, BS), line, 0.0), axis=1, keepdims=True)

    for r in range(n_rows):
        row = place[0] * n_rows + r
        w = jnp.where(lane < HALF, scale(2 * row), scale(2 * row + 1))
        wr = w * residual[pl.ds(row, 1), :]
        hi = wr.astype(jnp.bfloat16).astype(jnp.float32)
        mid = (wr - hi).astype(jnp.bfloat16).astype(jnp.float32)
        terms = stack_rows([hi, mid, wr - hi - mid])
        terms = jnp.concatenate([terms, jnp.zeros_like(terms)], axis=0).astype(jnp.bfloat16)
        copies[r].wait()

        def body(g):
            for s in range(PAIR):
                one = jac[r, g, s]
                scaled = (one.T.astype(jnp.float32) * w).astype(jnp.bfloat16)
                left = jnp.concatenate([scaled, terms], axis=0)
                out = lax.dot_general(left, one, (((1,), (0,)), ((), ())), preferred_element_type=jnp.float32)
                last = pltpu.roll(out[HALF:BS], HALF, 1)
                packed = jnp.where(upper, out[:HALF], last)
                diag = jnp.sum(jnp.where(lanes, last, 0.0), axis=0, keepdims=True)
                grad = jnp.sum(out[BS : BS + 8], axis=0, keepdims=True)
                main, tail = encode(packed, diag, grad)
                coded[r, g, s, :HALF] = main
                coded[r, g, s, HALF:] = tail

        loop(groups, unroll, body)
        done.append(pltpu.make_async_copy(coded.at[r], out_hbm.at[:, r], out_sem.at[r]))
        done[-1].start()
    for copy in done:
        copy.wait()


def place_kernel(unroll, targets, core, coded, own, other, acc):
    acc[...] = jnp.zeros_like(acc)

    def body(i):
        packed, diag, grad = decode(coded[i, :HALF], coded[i, HALF:])
        where = targets[i]
        acc[where, :HALF] += packed
        acc[where, HALF:] += stack_rows([diag, grad])

    loop(coded.shape[0], unroll, body)
    me = core[0]

    def split(i):
        own[i] = acc[2 * i + me]
        value = acc[2 * i + 1 - me]
        other[i, :HALF], other[i, HALF:] = encode(value[:HALF], value[HALF : HALF + 1], value[HALF + 1 : HALF + 2])

    loop(own.shape[0], unroll, split)


def halve_kernel(unroll, part, own, got, kept, coded):
    me = part[0]

    def body(i):
        mine, theirs = 2 * i + me, 2 * i + 1 - me
        packed, diag, grad = decode(got[mine, :HALF], got[mine, HALF:])
        kept[i, :HALF] = own[mine, :HALF] + packed
        kept[i, HALF:] = own[mine, HALF:] + stack_rows([diag, grad])
        packed, diag, grad = decode(got[theirs, :HALF], got[theirs, HALF:])
        tail = own[theirs, HALF:]
        coded[i, :HALF], coded[i, HALF:] = encode(own[theirs, :HALF] + packed, tail[0:1] + diag, tail[1:2] + grad)

    loop(coded.shape[0], unroll, body)


def recode_kernel(unroll, kept, got, coded):
    def body(i):
        packed, diag, grad = decode(got[i, :HALF], got[i, HALF:])
        tail = kept[i, HALF:]
        coded[i, :HALF], coded[i, HALF:] = encode(kept[i, :HALF] + packed, tail[0:1] + diag, tail[1:2] + grad)

    loop(coded.shape[0], unroll, body)


def finish_kernel(coded, diag_out, grad_out):
    packed = jnp.zeros((HALF, BS), jnp.float32)
    diag = jnp.zeros((1, BS), jnp.float32)
    grad = jnp.zeros((1, BS), jnp.float32)
    for i in range(coded.shape[0]):
        more = decode(coded[i, :HALF], coded[i, HALF:])
        packed, diag, grad = packed + more[0], diag + more[1], grad + more[2]
    whole = jnp.concatenate([packed, pltpu.roll(packed, HALF, 1)], axis=0)
    flipped = whole.T
    r, c = iota((BS, BS), 0), iota((BS, BS), 1)
    plain = ((r < HALF) & (c >= r)) | ((c >= HALF) & (c < r))
    on = (r == c) & (r >= HALF)
    diag_out[...] = jnp.where(on, pltpu.roll(diag, HALF, 1), jnp.where(plain, whole, flipped))
    grad_out[...] = grad


def call(body, outs, specs, out="v", vmem=32, scratch=(), flops=0, moved=0):
    spaces = {"v": pltpu.VMEM, "s": pltpu.SMEM, "h": pltpu.HBM}
    spec = pl.BlockSpec(memory_space=spaces[out])
    many = isinstance(outs, (list, tuple))
    return pl.pallas_call(
        body,
        out_shape=outs,
        in_specs=[pl.BlockSpec(memory_space=spaces[k]) for k in specs],
        out_specs=[spec] * len(outs) if many else spec,
        scratch_shapes=list(scratch),
        compiler_params=pltpu.CompilerParams(vmem_limit_bytes=vmem * 1024 * 1024),
        cost_estimate=pl.CostEstimate(flops=flops, bytes_accessed=moved, transcendentals=0),
    )


def shards(jac_blocks, col_blocks, residual, run_of_half, run_scale):
    f32, i16 = jnp.float32, jnp.int16
    slots = lax.axis_size("z") * 4
    n_rows, groups = jac_blocks.shape[:2]
    n_items = n_rows * groups * PAIR

    def index(name):
        return lax.axis_index(name).astype(jnp.int32).reshape(1)

    def shape(n, dtype):
        return jax.ShapeDtypeStruct((n, ROWS, BS), dtype)

    coded = call(
        functools.partial(products_kernel, 8),
        jax.ShapeDtypeStruct((groups, n_rows, PAIR, ROWS, BS), i16),
        "sshhh",
        out="h",
        vmem=60,
        scratch=[
            pltpu.VMEM(jac_blocks.shape, jnp.bfloat16),
            pltpu.VMEM((n_rows, groups, PAIR, ROWS, BS), i16),
            pltpu.VMEM((run_scale.shape[0] // BS, BS), jnp.bfloat16),
            pltpu.VMEM(residual.shape, f32),
            pltpu.VMEM((run_scale.shape[0] // BS, BS), f32),
            pltpu.SemaphoreType.DMA((n_rows,)),
            pltpu.SemaphoreType.DMA((n_rows,)),
            pltpu.SemaphoreType.DMA((2,)),
        ],
        flops=2 * n_items * BS**3,
        moved=n_items * BS * BS * 3,
    )(index("coef"), run_of_half, run_scale.reshape(-1, BS), residual, jac_blocks)
    landed = lax.all_to_all(coded, "coef", 0, 0, tiled=True).reshape(n_items, ROWS, BS)
    own, other = call(
        functools.partial(place_kernel, 8),
        [shape(slots // 2, f32), shape(slots // 2, i16)],
        "ssv",
        scratch=[pltpu.VMEM((slots, ROWS, BS), f32)],
    )(col_blocks.reshape(-1), index("core"), landed)
    got = lax.ppermute(other, "core", [(0, 1), (1, 0)])
    kept, coded = call(
        functools.partial(halve_kernel, 8), [shape(slots // 4, f32), shape(slots // 4, i16)], "svv"
    )(index("yh"), own, got)
    got = lax.ppermute(coded, "yh", [(0, 1), (1, 0)])
    coded = call(functools.partial(recode_kernel, 8), shape(slots // 4, i16), "vv")(kept, got)
    landed = lax.all_to_all(coded, "z", 0, 0, tiled=True)
    diag, grad = call(
        finish_kernel, [jax.ShapeDtypeStruct((BS, BS), f32), jax.ShapeDtypeStruct((1, BS), f32)], "v"
    )(landed)
    return diag.reshape(1, 1, BS, BS), grad.reshape(1, 1, BS)


def solution(mesh):
    fine = Mesh(mesh.devices.reshape(-1, 2, 2, mesh.devices.shape[1]), ("z", "yh", "core", "coef"))
    batch = ("z", "yh", "core")
    in_specs = (
        P(batch + ("coef",), None, None, None, None),
        P("coef", batch, None),
        P(batch, None),
        P(batch),
        P(),
    )
    out_specs = (P("coef", batch, None, None), P("coef", batch, None))
    return jax.shard_map(shards, mesh=fine, in_specs=in_specs, out_specs=out_specs, check_vma=False)
```

```python
import functools
import math

import jax
import jax.numpy as jnp
from jax import lax
from jax.experimental import pallas as pl
from jax.experimental.pallas import tpu as pltpu
from jax.sharding import Mesh
from jax.sharding import PartitionSpec as P

BS = 128
HALF = BS // 2
PAIR = 2
ROWS = HALF + 8
FULL = 32000.0
STEPS = 16.0
TINY = 1e-30
PER = STEPS / 0.6931471805599453


def iota(shape, dim):
    return lax.broadcasted_iota(jnp.int32, shape, dim)


def stack_rows(rows):
    sub = iota((8, BS), 0)
    out = jnp.zeros((8, BS), jnp.float32)
    for k, row in enumerate(rows):
        out = jnp.where(sub == k, row, out)
    return out


def to_int16(x):
    return jnp.round(x).astype(jnp.int32).astype(jnp.int16)


def loop(n, unroll, body):
    unroll = math.gcd(n, unroll)

    def step(block, carry):
        for j in range(unroll):
            body(block * unroll + j)
        return carry

    lax.fori_loop(0, n // unroll, step, 0)


def encode(packed, diag, grad):
    big = jnp.maximum(jnp.max(jnp.abs(packed), axis=0, keepdims=True), jnp.maximum(jnp.abs(diag), TINY))
    big_g = jnp.maximum(jnp.abs(grad), TINY)
    code = jnp.ceil(jnp.log(big) * PER)
    code_g = jnp.ceil(jnp.log(big_g) * PER)
    inv = jnp.exp2(code * (-1.0 / STEPS)) * FULL
    inv_g = jnp.exp2(code_g * (-1.0 / STEPS)) * FULL
    g = grad * inv_g
    g_hi = jnp.round(g)
    g_lo = (g - g_hi) * FULL
    return to_int16(packed * inv), to_int16(stack_rows([diag * inv, code, code_g, g_hi, g_lo]))


def decode(main, tail):
    tail = tail.astype(jnp.int32).astype(jnp.float32)
    scale = jnp.exp2(tail[1:2] * (1.0 / STEPS)) * (1.0 / FULL)
    scale_g = jnp.exp2(tail[2:3] * (1.0 / STEPS)) * (1.0 / FULL)
    packed = main.astype(jnp.int32).astype(jnp.float32) * scale
    return packed, tail[0:1] * scale, (tail[3:4] + tail[4:5] * (1.0 / FULL)) * scale_g


def products_kernel(unroll, place, runs, scales_hbm, residual_hbm, jac_hbm, out_hbm, jac, coded, scales, residual, table, sem, out_sem, aux_sem):
    n_rows, groups = jac_hbm.shape[:2]
    copies = [pltpu.make_async_copy(jac_hbm.at[r], jac.at[r], sem.at[r]) for r in range(n_rows)]
    aux = [
        pltpu.make_async_copy(scales_hbm, scales, aux_sem.at[0]),
        pltpu.make_async_copy(residual_hbm, residual, aux_sem.at[1]),
    ]
    for copy in aux + copies:
        copy.start()
    done = []
    for copy in aux:
        copy.wait()
    table[...] = scales[...].astype(jnp.float32)
    upper = iota((HALF, BS), 1) >= iota((HALF, BS), 0)
    lanes = iota((HALF, BS), 1) == iota((HALF, BS), 0)
    lane = iota((1, BS), 1)

    def scale(half):
        run = runs[half]
        line = table[pl.ds(lax.div(run, BS), 1), :]
        return jnp.sum(jnp.where(lane == lax.rem(run, BS), line, 0.0), axis=1, keepdims=True)

    for r in range(n_rows):
        row = place[0] * n_rows + r
        w = jnp.where(lane < HALF, scale(2 * row), scale(2 * row + 1))
        wr = w * residual[pl.ds(row, 1), :]
        hi = wr.astype(jnp.bfloat16).astype(jnp.float32)
        mid = (wr - hi).astype(jnp.bfloat16).astype(jnp.float32)
        terms = stack_rows([hi, mid, wr - hi - mid])
        terms = jnp.concatenate([terms, jnp.zeros_like(terms)], axis=0).astype(jnp.bfloat16)
        copies[r].wait()

        def body(g):
            for s in range(PAIR):
                one = jac[r, g, s]
                scaled = (one.T.astype(jnp.float32) * w).astype(jnp.bfloat16)
                left = jnp.concatenate([scaled, terms], axis=0)
                out = lax.dot_general(left, one, (((1,), (0,)), ((), ())), preferred_element_type=jnp.float32)
                last = pltpu.roll(out[HALF:BS], HALF, 1)
                packed = jnp.where(upper, out[:HALF], last)
                diag = jnp.sum(jnp.where(lanes, last, 0.0), axis=0, keepdims=True)
                grad = jnp.sum(out[BS : BS + 8], axis=0, keepdims=True)
                main, tail = encode(packed, diag, grad)
                coded[r, g, s, :HALF] = main
                coded[r, g, s, HALF:] = tail

        loop(groups, unroll, body)
        done.append(pltpu.make_async_copy(coded.at[r], out_hbm.at[:, r], out_sem.at[r]))
        done[-1].start()
    for copy in done:
        copy.wait()


def place_kernel(unroll, targets, core, coded, own, other, acc):
    acc[...] = jnp.zeros_like(acc)

    def body(i):
        packed, diag, grad = decode(coded[i, :HALF], coded[i, HALF:])
        where = targets[i]
        acc[where, :HALF] += packed
        acc[where, HALF:] += stack_rows([diag, grad])

    loop(coded.shape[0], unroll, body)
    me = core[0]

    def split(i):
        own[i] = acc[2 * i + me]
        value = acc[2 * i + 1 - me]
        other[i, :HALF], other[i, HALF:] = encode(value[:HALF], value[HALF : HALF + 1], value[HALF + 1 : HALF + 2])

    loop(own.shape[0], unroll, split)


def join_kernel(unroll, own, got, coded):
    near = coded.shape[0]

    def body(i):
        packed, diag, grad = decode(got[i, :HALF], got[i, HALF:])
        tail = own[i, HALF:]
        main, tail = encode(own[i, :HALF] + packed, tail[0:1] + diag, tail[1:2] + grad)
        to, slot = lax.rem(i, near), lax.div(i, near)
        coded[to, slot, :HALF] = main
        coded[to, slot, HALF:] = tail

    loop(own.shape[0], unroll, body)


def gather_sum(coded, i):
    total = decode(coded[0, i, :HALF], coded[0, i, HALF:])
    for k in range(1, coded.shape[0]):
        more = decode(coded[k, i, :HALF], coded[k, i, HALF:])
        total = [x + y for x, y in zip(total, more)]
    return total


def recode_kernel(unroll, got, coded):
    def body(i):
        coded[i, :HALF], coded[i, HALF:] = encode(*gather_sum(got, i))

    loop(coded.shape[0], unroll, body)


def finish_kernel(coded, diag_out, grad_out):
    packed, diag, grad = gather_sum(coded, 0)
    whole = jnp.concatenate([packed, pltpu.roll(packed, HALF, 1)], axis=0)
    flipped = whole.T
    r, c = iota((BS, BS), 0), iota((BS, BS), 1)
    plain = ((r < HALF) & (c >= r)) | ((c >= HALF) & (c < r))
    on = (r == c) & (r >= HALF)
    diag_out[...] = jnp.where(on, pltpu.roll(diag, HALF, 1), jnp.where(plain, whole, flipped))
    grad_out[...] = grad


def call(body, outs, specs, out="v", vmem=32, scratch=(), flops=0, moved=0):
    spaces = {"v": pltpu.VMEM, "s": pltpu.SMEM, "h": pltpu.HBM}
    spec = pl.BlockSpec(memory_space=spaces[out])
    many = isinstance(outs, (list, tuple))
    return pl.pallas_call(
        body,
        out_shape=outs,
        in_specs=[pl.BlockSpec(memory_space=spaces[k]) for k in specs],
        out_specs=[spec] * len(outs) if many else spec,
        scratch_shapes=list(scratch),
        compiler_params=pltpu.CompilerParams(vmem_limit_bytes=vmem * 1024 * 1024),
        cost_estimate=pl.CostEstimate(flops=flops, bytes_accessed=moved, transcendentals=0),
    )


def shards(jac_blocks, col_blocks, residual, run_of_half, run_scale):
    f32, i16 = jnp.float32, jnp.int16
    far = lax.axis_size("zq")
    slots = far * 8
    n_rows, groups = jac_blocks.shape[:2]
    n_items = n_rows * groups * PAIR

    def index(name):
        return lax.axis_index(name).astype(jnp.int32).reshape(1)

    def shape(n, dtype):
        return jax.ShapeDtypeStruct((n, ROWS, BS), dtype)

    coded = call(
        functools.partial(products_kernel, 8),
        jax.ShapeDtypeStruct((groups, n_rows, PAIR, ROWS, BS), i16),
        "sshhh",
        out="h",
        vmem=60,
        scratch=[
            pltpu.VMEM(jac_blocks.shape, jnp.bfloat16),
            pltpu.VMEM((n_rows, groups, PAIR, ROWS, BS), i16),
            pltpu.VMEM((run_scale.shape[0] // BS, BS), jnp.bfloat16),
            pltpu.VMEM(residual.shape, f32),
            pltpu.VMEM((run_scale.shape[0] // BS, BS), f32),
            pltpu.SemaphoreType.DMA((n_rows,)),
            pltpu.SemaphoreType.DMA((n_rows,)),
            pltpu.SemaphoreType.DMA((2,)),
        ],
        flops=2 * n_items * BS**3,
        moved=n_items * BS * BS * 3,
    )(index("coef"), run_of_half, run_scale.reshape(-1, BS), residual, jac_blocks)
    landed = lax.all_to_all(coded, "coef", 0, 0, tiled=True).reshape(n_items, ROWS, BS)
    own, other = call(
        functools.partial(place_kernel, 8),
        [shape(slots // 2, f32), shape(slots // 2, i16)],
        "ssv",
        scratch=[pltpu.VMEM((slots, ROWS, BS), f32)],
    )(col_blocks.reshape(-1), index("core"), landed)
    got = lax.ppermute(other, "core", [(0, 1), (1, 0)])
    near = slots // 2 // far
    coded = call(
        functools.partial(join_kernel, 8), jax.ShapeDtypeStruct((near, far, ROWS, BS), i16), "vv"
    )(own, got)
    landed = lax.all_to_all(coded, ("z0", "yh"), 0, 0, tiled=True)
    coded = call(functools.partial(recode_kernel, 8), shape(far, i16), "v")(landed)
    landed = lax.all_to_all(coded, "zq", 0, 0, tiled=True).reshape(far, 1, ROWS, BS)
    diag, grad = call(
        finish_kernel, [jax.ShapeDtypeStruct((BS, BS), f32), jax.ShapeDtypeStruct((1, BS), f32)], "v"
    )(landed)
    return diag.reshape(1, 1, BS, BS), grad.reshape(1, 1, BS)


def solution(mesh):
    fine = Mesh(mesh.devices.reshape(-1, 2, 2, 2, mesh.devices.shape[1]), ("zq", "z0", "yh", "core", "coef"))
    batch = ("zq", "z0", "yh", "core")
    in_specs = (
        P(batch + ("coef",), None, None, None, None),
        P("coef", batch, None),
        P(batch, None),
        P(batch),
        P(),
    )
    out_specs = (P("coef", batch, None, None), P("coef", batch, None))
    return jax.shard_map(shards, mesh=fine, in_specs=in_specs, out_specs=out_specs, check_vma=False)
```

```python
import functools
import math

import jax
import jax.numpy as jnp
from jax import lax
from jax.experimental import pallas as pl
from jax.experimental.pallas import tpu as pltpu
from jax.sharding import Mesh
from jax.sharding import PartitionSpec as P

BS = 128
HALF = BS // 2
PAIR = 2
ROWS = HALF + 8
FULL = 32000.0
STEPS = 16.0
TINY = 1e-30
PER = STEPS / 0.6931471805599453


def iota(shape, dim):
    return lax.broadcasted_iota(jnp.int32, shape, dim)


def stack_rows(rows):
    sub = iota((8, BS), 0)
    out = jnp.zeros((8, BS), jnp.float32)
    for k, row in enumerate(rows):
        out = jnp.where(sub == k, row, out)
    return out


def to_int16(x):
    return jnp.round(x).astype(jnp.int32).astype(jnp.int16)


def loop(n, unroll, body):
    unroll = math.gcd(n, unroll)

    def step(block, carry):
        for j in range(unroll):
            body(block * unroll + j)
        return carry

    lax.fori_loop(0, n // unroll, step, 0)


def encode(packed, diag, grad):
    big = jnp.maximum(jnp.max(jnp.abs(packed), axis=0, keepdims=True), jnp.maximum(jnp.abs(diag), TINY))
    big_g = jnp.maximum(jnp.abs(grad), TINY)
    code = jnp.ceil(jnp.log(big) * PER)
    code_g = jnp.ceil(jnp.log(big_g) * PER)
    inv = jnp.exp2(code * (-1.0 / STEPS)) * FULL
    inv_g = jnp.exp2(code_g * (-1.0 / STEPS)) * FULL
    g = grad * inv_g
    g_hi = jnp.round(g)
    g_lo = (g - g_hi) * FULL
    return to_int16(packed * inv), to_int16(stack_rows([diag * inv, code, code_g, g_hi, g_lo]))


def decode(main, tail):
    tail = tail.astype(jnp.int32).astype(jnp.float32)
    scale = jnp.exp2(tail[1:2] * (1.0 / STEPS)) * (1.0 / FULL)
    scale_g = jnp.exp2(tail[2:3] * (1.0 / STEPS)) * (1.0 / FULL)
    packed = main.astype(jnp.int32).astype(jnp.float32) * scale
    return packed, tail[0:1] * scale, (tail[3:4] + tail[4:5] * (1.0 / FULL)) * scale_g


def products_kernel(unroll, runs_hbm, scales_hbm, residual_hbm, jac_hbm, coded, jac, runs, scales, residual, table, sem, aux_sem):
    n_rows, groups = jac_hbm.shape[:2]
    aux = [
        pltpu.make_async_copy(runs_hbm, runs, aux_sem.at[0]),
        pltpu.make_async_copy(scales_hbm, scales, aux_sem.at[1]),
        pltpu.make_async_copy(residual_hbm, residual, aux_sem.at[2]),
    ]
    copies = [pltpu.make_async_copy(jac_hbm.at[r], jac.at[r], sem.at[r]) for r in range(n_rows)]
    for copy in aux + copies:
        copy.start()
    first = lax.axis_index("coef") * n_rows
    upper = iota((HALF, BS), 1) >= iota((HALF, BS), 0)
    lanes = iota((HALF, BS), 1) == iota((HALF, BS), 0)
    lane = iota((1, BS), 1)
    for copy in aux:
        copy.wait()
    table[...] = scales[...].astype(jnp.float32)

    def scale(half):
        run = runs[half]
        line = table[pl.ds(lax.div(run, BS), 1), :]
        return jnp.sum(jnp.where(lane == lax.rem(run, BS), line, 0.0), axis=1, keepdims=True)

    weights, terms = [], []
    for r in range(n_rows):
        row = first + r
        w = jnp.where(lane < HALF, scale(2 * row), scale(2 * row + 1))
        wr = w * residual[pl.ds(row, 1), :]
        hi = wr.astype(jnp.bfloat16).astype(jnp.float32)
        mid = (wr - hi).astype(jnp.bfloat16).astype(jnp.float32)
        split = stack_rows([hi, mid, wr - hi - mid])
        weights.append(w)
        terms.append(jnp.concatenate([split, jnp.zeros_like(split)], axis=0).astype(jnp.bfloat16))

    for r in range(n_rows):
        copies[r].wait()

        def body(g):
            for s in range(PAIR):
                one = jac[r, g, s]
                scaled = (one.T.astype(jnp.float32) * weights[r]).astype(jnp.bfloat16)
                left = jnp.concatenate([scaled, terms[r]], axis=0)
                out = lax.dot_general(left, one, (((1,), (0,)), ((), ())), preferred_element_type=jnp.float32)
                last = pltpu.roll(out[HALF:BS], HALF, 1)
                packed = jnp.where(upper, out[:HALF], last)
                diag = jnp.sum(jnp.where(lanes, last, 0.0), axis=0, keepdims=True)
                grad = jnp.sum(out[BS : BS + 8], axis=0, keepdims=True)
                main, tail = encode(packed, diag, grad)
                coded[g, r, s, :HALF] = main
                coded[g, r, s, HALF:] = tail

        loop(groups, unroll, body)


def place_kernel(unroll, targets_hbm, coded, acc, other, targets, sem):
    copy = pltpu.make_async_copy(targets_hbm, targets, sem)
    copy.start()
    acc[...] = jnp.zeros_like(acc)
    copy.wait()

    def body(i):
        packed, diag, grad = decode(coded[i, :HALF], coded[i, HALF:])
        where = targets[lax.rem(i, PAIR), lax.div(i, PAIR)]
        acc[where, :HALF] += packed
        acc[where, HALF:] += stack_rows([diag, grad])

    loop(coded.shape[0], unroll, body)
    theirs = 1 - lax.axis_index("core")

    def split(i):
        value = acc[2 * i + theirs]
        other[i, :HALF], other[i, HALF:] = encode(value[:HALF], value[HALF : HALF + 1], value[HALF + 1 : HALF + 2])

    loop(other.shape[0], unroll, split)


def join_kernel(unroll, acc, got, coded):
    near = coded.shape[0]
    me = lax.axis_index("core")

    def body(i):
        packed, diag, grad = decode(got[i, :HALF], got[i, HALF:])
        mine = 2 * i + me
        tail = acc[mine, HALF:]
        main, tail = encode(acc[mine, :HALF] + packed, tail[0:1] + diag, tail[1:2] + grad)
        to, slot = lax.rem(i, near), lax.div(i, near)
        coded[to, slot, :HALF] = main
        coded[to, slot, HALF:] = tail

    loop(got.shape[0], unroll, body)


def gather_sum(coded, i):
    total = decode(coded[0, i, :HALF], coded[0, i, HALF:])
    for k in range(1, coded.shape[0]):
        more = decode(coded[k, i, :HALF], coded[k, i, HALF:])
        total = [x + y for x, y in zip(total, more)]
    return total


def recode_kernel(unroll, got, coded):
    def body(i):
        coded[i, :HALF], coded[i, HALF:] = encode(*gather_sum(got, i))

    loop(coded.shape[0], unroll, body)


def finish_kernel(coded, diag_out, grad_out):
    packed, diag, grad = gather_sum(coded, 0)
    whole = jnp.concatenate([packed, pltpu.roll(packed, HALF, 1)], axis=0)
    flipped = whole.T
    r, c = iota((BS, BS), 0), iota((BS, BS), 1)
    plain = ((r < HALF) & (c >= r)) | ((c >= HALF) & (c < r))
    on = (r == c) & (r >= HALF)
    diag_out[...] = jnp.where(on, pltpu.roll(diag, HALF, 1), jnp.where(plain, whole, flipped))
    grad_out[...] = grad


def call(body, outs, specs, out="v", vmem=32, scratch=(), flops=0, moved=0):
    spaces = {"v": pltpu.VMEM, "s": pltpu.SMEM, "h": pltpu.HBM}
    spec = pl.BlockSpec(memory_space=spaces[out])
    many = isinstance(outs, (list, tuple))
    return pl.pallas_call(
        body,
        out_shape=outs,
        in_specs=[pl.BlockSpec(memory_space=spaces[k]) for k in specs],
        out_specs=[spec] * len(outs) if many else spec,
        scratch_shapes=list(scratch),
        compiler_params=pltpu.CompilerParams(vmem_limit_bytes=vmem * 1024 * 1024),
        cost_estimate=pl.CostEstimate(flops=flops, bytes_accessed=moved, transcendentals=0),
    )


def shards(jac_blocks, col_blocks, residual, run_of_half, run_scale):
    f32, i16 = jnp.float32, jnp.int16
    far = lax.axis_size("zq")
    slots = far * 8
    n_rows, groups = jac_blocks.shape[:2]
    n_items = n_rows * groups * PAIR

    def shape(n, dtype):
        return jax.ShapeDtypeStruct((n, ROWS, BS), dtype)

    targets = col_blocks[0].T
    coded = call(
        functools.partial(products_kernel, 8),
        jax.ShapeDtypeStruct((groups, n_rows, PAIR, ROWS, BS), i16),
        "hhhh",
        vmem=60,
        scratch=[
            pltpu.VMEM(jac_blocks.shape, jnp.bfloat16),
            pltpu.SMEM(run_of_half.shape, jnp.int32),
            pltpu.VMEM((run_scale.shape[0] // BS, BS), jnp.bfloat16),
            pltpu.VMEM(residual.shape, f32),
            pltpu.VMEM((run_scale.shape[0] // BS, BS), f32),
            pltpu.SemaphoreType.DMA((n_rows,)),
            pltpu.SemaphoreType.DMA((3,)),
        ],
        flops=2 * n_items * BS**3,
        moved=n_items * BS * BS * 3,
    )(run_of_half, run_scale.reshape(-1, BS), residual, jac_blocks)
    landed = lax.all_to_all(coded, "coef", 0, 0, tiled=True).reshape(n_items, ROWS, BS)
    acc, other = call(
        functools.partial(place_kernel, 8),
        [shape(slots, f32), shape(slots // 2, i16)],
        "hv",
        scratch=[pltpu.SMEM(targets.shape, jnp.int32), pltpu.SemaphoreType.DMA],
    )(targets, landed)
    got = lax.ppermute(other, "core", [(0, 1), (1, 0)])
    near = slots // 2 // far
    coded = call(
        functools.partial(join_kernel, 8), jax.ShapeDtypeStruct((near, far, ROWS, BS), i16), "vv"
    )(acc, got)
    landed = lax.all_to_all(coded, ("z0", "yh"), 0, 0, tiled=True)
    coded = call(functools.partial(recode_kernel, 8), shape(far, i16), "v")(landed)
    landed = lax.all_to_all(coded, "zq", 0, 0, tiled=True).reshape(far, 1, ROWS, BS)
    diag, grad = call(
        finish_kernel, [jax.ShapeDtypeStruct((BS, BS), f32), jax.ShapeDtypeStruct((1, BS), f32)], "v"
    )(landed)
    return diag.reshape(1, 1, BS, BS), grad.reshape(1, 1, BS)


def solution(mesh):
    fine = Mesh(mesh.devices.reshape(-1, 2, 2, 2, mesh.devices.shape[1]), ("zq", "z0", "yh", "core", "coef"))
    batch = ("zq", "z0", "yh", "core")
    in_specs = (
        P(batch + ("coef",), None, None, None, None),
        P("coef", batch, None),
        P(batch, None),
        P(batch),
        P(),
    )
    out_specs = (P("coef", batch, None, None), P("coef", batch, None))
    return jax.shard_map(shards, mesh=fine, in_specs=in_specs, out_specs=out_specs, check_vma=False)
```

```python
import functools
import math

import jax
import jax.numpy as jnp
from jax import lax
from jax.experimental import pallas as pl
from jax.experimental.pallas import tpu as pltpu
from jax.sharding import Mesh
from jax.sharding import PartitionSpec as P

BS = 128
HALF = BS // 2
PAIR = 2
ROWS = HALF + 8
DUO = 2 * HALF + 8
FULL = 32000.0
STEPS = 16.0
TINY = 1e-30
PER = STEPS / 0.6931471805599453


def iota(shape, dim):
    return lax.broadcasted_iota(jnp.int32, shape, dim)


def stack_rows(rows):
    sub = iota((8, BS), 0)
    out = jnp.zeros((8, BS), jnp.float32)
    for k, row in enumerate(rows):
        out = jnp.where(sub == k, row, out)
    return out


def to_int16(x):
    return jnp.round(x).astype(jnp.int32).astype(jnp.int16)


def loop(n, unroll, body):
    unroll = math.gcd(n, unroll)

    def step(block, carry):
        for j in range(unroll):
            body(block * unroll + j)
        return carry

    lax.fori_loop(0, n // unroll, step, 0)


def encode(packed, diag, grad):
    big = jnp.maximum(jnp.max(jnp.abs(packed), axis=0, keepdims=True), jnp.maximum(jnp.abs(diag), TINY))
    big_g = jnp.maximum(jnp.maximum(jnp.abs(grad), pltpu.roll(jnp.abs(grad), HALF, 1)), TINY)
    code = jnp.ceil(jnp.log(big) * PER)
    code_g = jnp.ceil(jnp.log(big_g) * PER)
    inv = jnp.exp2(code * (-1.0 / STEPS)) * FULL
    inv_g = jnp.exp2(code_g * (-1.0 / STEPS)) * FULL
    g = grad * inv_g
    g_hi = jnp.round(g)
    g_lo = (g - g_hi) * FULL
    first = jnp.where(iota((1, BS), 1) < HALF, diag * inv, code_g)
    return packed * inv, [first, code, g_hi, g_lo]


def put_two(coded, at, two):
    for k, (main, _) in enumerate(two):
        coded[at + (pl.ds(k * HALF, HALF),)] = to_int16(main)
    coded[at + (pl.ds(2 * HALF, 8),)] = to_int16(stack_rows(two[0][1] + two[1][1]))


def decode(main, tail):
    low = iota((1, BS), 1) < HALF
    code_g = jnp.where(low, pltpu.roll(tail[0:1], HALF, 1), tail[0:1])
    scale = jnp.exp2(tail[1:2] * (1.0 / STEPS)) * (1.0 / FULL)
    scale_g = jnp.exp2(code_g * (1.0 / STEPS)) * (1.0 / FULL)
    packed = main.astype(jnp.int32).astype(jnp.float32) * scale
    return packed, jnp.where(low, tail[0:1] * scale, 0.0), (tail[2:3] + tail[3:4] * (1.0 / FULL)) * scale_g


def get_two(coded, at):
    tail = coded[at + (pl.ds(2 * HALF, 8),)].astype(jnp.int32).astype(jnp.float32)
    return [decode(coded[at + (pl.ds(k * HALF, HALF),)], tail[4 * k : 4 * k + 4]) for k in range(2)]


def products_kernel(unroll, runs_hbm, scales_hbm, residual_hbm, jac_hbm, coded, jac, runs, scales, residual, table, sem, aux_sem):
    n_rows, groups = jac_hbm.shape[:2]
    aux = [
        pltpu.make_async_copy(runs_hbm, runs, aux_sem.at[0]),
        pltpu.make_async_copy(scales_hbm, scales, aux_sem.at[1]),
        pltpu.make_async_copy(residual_hbm, residual, aux_sem.at[2]),
    ]
    copies = [pltpu.make_async_copy(jac_hbm.at[r], jac.at[r], sem.at[r]) for r in range(n_rows)]
    for copy in aux + copies:
        copy.start()
    first = lax.axis_index("coef") * n_rows
    upper = iota((HALF, BS), 1) >= iota((HALF, BS), 0)
    lanes = iota((HALF, BS), 1) == iota((HALF, BS), 0)
    lane = iota((1, BS), 1)
    for copy in aux:
        copy.wait()
    table[...] = scales[...].astype(jnp.float32)

    def scale(half):
        run = runs[half]
        line = table[pl.ds(lax.div(run, BS), 1), :]
        return jnp.sum(jnp.where(lane == lax.rem(run, BS), line, 0.0), axis=1, keepdims=True)

    weights, terms = [], []
    for r in range(n_rows):
        row = first + r
        w = jnp.where(lane < HALF, scale(2 * row), scale(2 * row + 1))
        wr = w * residual[pl.ds(row, 1), :]
        hi = wr.astype(jnp.bfloat16).astype(jnp.float32)
        mid = (wr - hi).astype(jnp.bfloat16).astype(jnp.float32)
        split = stack_rows([hi, mid, wr - hi - mid])
        weights.append(jnp.broadcast_to(w, (BS, BS)).astype(jnp.bfloat16))
        terms.append(jnp.concatenate([split, jnp.zeros_like(split)], axis=0).astype(jnp.bfloat16))

    for r in range(n_rows):
        copies[r].wait()

        def body(g):
            two = []
            for s in range(PAIR):
                one = jac[r, g, s]
                scaled = one.T * weights[r]
                left = jnp.concatenate([scaled, terms[r]], axis=0)
                out = lax.dot_general(left, one, (((1,), (0,)), ((), ())), preferred_element_type=jnp.float32)
                last = pltpu.roll(out[HALF:BS], HALF, 1)
                packed = jnp.where(upper, out[:HALF], last)
                diag = jnp.sum(jnp.where(lanes, last, 0.0), axis=0, keepdims=True)
                grad = jnp.sum(out[BS : BS + 8], axis=0, keepdims=True)
                two.append(encode(packed, diag, grad))
            put_two(coded, (g, r), two)

        loop(groups, unroll, body)


def place_kernel(unroll, targets_hbm, coded, acc, other, targets, sem):
    copy = pltpu.make_async_copy(targets_hbm, targets, sem)
    copy.start()
    acc[...] = jnp.zeros_like(acc)
    copy.wait()

    def body(row):
        for s, (packed, diag, grad) in enumerate(get_two(coded, (row,))):
            where = targets[s, row]
            acc[where, :HALF] += packed
            acc[where, HALF:] += stack_rows([diag, grad])

    loop(coded.shape[0], unroll, body)
    theirs = 1 - lax.axis_index("core")

    def split(i):
        put_two(other, (i,), [encode_slot(acc[2 * (2 * i + k) + theirs]) for k in range(2)])

    loop(other.shape[0], unroll, split)


def encode_slot(value):
    return encode(value[:HALF], value[HALF : HALF + 1], value[HALF + 1 : HALF + 2])


def join_kernel(unroll, acc, got, coded):
    me = lax.axis_index("core")

    def body(i):
        far, bit = lax.div(i, 2), lax.rem(i, 2)
        new = ([], [])
        for k in range(2):
            at = 4 * far + 2 * k + bit
            for y, more in enumerate(get_two(got, (at,))):
                mine = acc[2 * (2 * at + y) + me]
                parts = mine[:HALF], mine[HALF : HALF + 1], mine[HALF + 1 : HALF + 2]
                new[y].append(encode(*[p + q for p, q in zip(parts, more)]))
        for y in range(2):
            put_two(coded, (2 * bit + y, far), new[y])

    loop(got.shape[0] // 2, unroll, body)


def add_up(several):
    total = several[0]
    for more in several[1:]:
        total = [x + y for x, y in zip(total, more)]
    return total


def recode_kernel(unroll, got, coded):
    def body(i):
        several = [get_two(got, (k, i)) for k in range(got.shape[0])]
        for k in range(2):
            main, tail = encode(*add_up([two[k] for two in several]))
            coded[2 * i + k, :HALF] = to_int16(main)
            coded[2 * i + k, HALF:] = to_int16(stack_rows(tail))

    loop(got.shape[1], unroll, body)


def finish_kernel(coded, diag_out, grad_out):
    packed, diag, grad = add_up(
        [decode(coded[k, :HALF], coded[k, HALF:].astype(jnp.int32).astype(jnp.float32)) for k in range(coded.shape[0])]
    )
    whole = jnp.concatenate([packed, pltpu.roll(packed, HALF, 1)], axis=0)
    flipped = whole.T
    r, c = iota((BS, BS), 0), iota((BS, BS), 1)
    plain = ((r < HALF) & (c >= r)) | ((c >= HALF) & (c < r))
    on = (r == c) & (r >= HALF)
    diag_out[...] = jnp.where(on, pltpu.roll(diag, HALF, 1), jnp.where(plain, whole, flipped))
    grad_out[...] = grad


def call(body, outs, specs, out="v", vmem=32, scratch=(), flops=0, moved=0):
    spaces = {"v": pltpu.VMEM, "s": pltpu.SMEM, "h": pltpu.HBM}
    spec = pl.BlockSpec(memory_space=spaces[out])
    many = isinstance(outs, (list, tuple))
    return pl.pallas_call(
        body,
        out_shape=outs,
        in_specs=[pl.BlockSpec(memory_space=spaces[k]) for k in specs],
        out_specs=[spec] * len(outs) if many else spec,
        scratch_shapes=list(scratch),
        compiler_params=pltpu.CompilerParams(vmem_limit_bytes=vmem * 1024 * 1024),
        cost_estimate=pl.CostEstimate(flops=flops, bytes_accessed=moved, transcendentals=0),
    )


def shards(jac_blocks, col_blocks, residual, run_of_half, run_scale):
    f32, i16 = jnp.float32, jnp.int16
    far = lax.axis_size("zq")
    slots = far * 8
    n_rows, groups = jac_blocks.shape[:2]
    n_items = n_rows * groups * PAIR

    def shape(n, dtype):
        return jax.ShapeDtypeStruct((n, ROWS, BS), dtype)

    targets = col_blocks[0].T
    coded = call(
        functools.partial(products_kernel, 8),
        jax.ShapeDtypeStruct((groups, n_rows, DUO, BS), i16),
        "hhhh",
        vmem=32,
        scratch=[
            pltpu.VMEM(jac_blocks.shape, jnp.bfloat16),
            pltpu.SMEM(run_of_half.shape, jnp.int32),
            pltpu.VMEM((run_scale.shape[0] // BS, BS), jnp.bfloat16),
            pltpu.VMEM(residual.shape, f32),
            pltpu.VMEM((run_scale.shape[0] // BS, BS), f32),
            pltpu.SemaphoreType.DMA((n_rows,)),
            pltpu.SemaphoreType.DMA((3,)),
        ],
        flops=2 * n_items * BS**3,
        moved=n_items * BS * BS * 3,
    )(*[pltpu.with_memory_space_constraint(x, pltpu.HBM) for x in (run_of_half, run_scale.reshape(-1, BS), residual, jac_blocks)])
    landed = lax.all_to_all(coded, "coef", 0, 0, tiled=True).reshape(n_items // PAIR, DUO, BS)
    acc, other = call(
        functools.partial(place_kernel, 16),
        [shape(slots, f32), jax.ShapeDtypeStruct((slots // 4, DUO, BS), i16)],
        "hv",
        scratch=[pltpu.SMEM(targets.shape, jnp.int32), pltpu.SemaphoreType.DMA],
    )(targets, landed)
    got = lax.ppermute(other, "core", [(0, 1), (1, 0)])
    near = slots // 2 // far
    coded = call(
        functools.partial(join_kernel, 16), jax.ShapeDtypeStruct((near, far // 2, DUO, BS), i16), "vv"
    )(acc, got)
    landed = lax.all_to_all(coded, ("z0", "yh"), 0, 0, tiled=True)
    coded = call(functools.partial(recode_kernel, 8), shape(far, i16), "v")(landed)
    landed = lax.all_to_all(coded, "zq", 0, 0, tiled=True)
    diag, grad = call(
        finish_kernel, [jax.ShapeDtypeStruct((BS, BS), f32), jax.ShapeDtypeStruct((1, BS), f32)], "v"
    )(landed)
    return diag.reshape(1, 1, BS, BS), grad.reshape(1, 1, BS)


def solution(mesh):
    fine = Mesh(mesh.devices.reshape(-1, 2, 2, 2, mesh.devices.shape[1]), ("zq", "z0", "yh", "core", "coef"))
    batch = ("zq", "z0", "yh", "core")
    in_specs = (
        P(batch + ("coef",), None, None, None, None),
        P("coef", batch, None),
        P(batch, None),
        P(batch),
        P(),
    )
    out_specs = (P("coef", batch, None, None), P("coef", batch, None))
    return jax.shard_map(shards, mesh=fine, in_specs=in_specs, out_specs=out_specs, check_vma=False)
```

```python
import functools
import math

import jax
import jax.numpy as jnp
from jax import lax
from jax.experimental import pallas as pl
from jax.experimental.pallas import tpu as pltpu
from jax.sharding import Mesh
from jax.sharding import PartitionSpec as P

BS = 128
HALF = BS // 2
PAIR = 2
ROWS = HALF + 8
DUO = 2 * HALF + 8
FULL = 32000.0
STEPS = 16.0
TINY = 1e-30
PER = STEPS / 0.6931471805599453


ORDER = [4, 0, 5, 1, 6, 2, 7, 3]


def iota(shape, dim):
    return lax.broadcasted_iota(jnp.int32, shape, dim)


def stack_rows(rows):
    sub = iota((8, BS), 0)
    out = jnp.zeros((8, BS), jnp.float32)
    for k, row in enumerate(rows):
        out = jnp.where(sub == k, row, out)
    return out


def to_int16(x):
    return jnp.round(x).astype(jnp.int32).astype(jnp.int16)


def loop(n, unroll, body):
    unroll = math.gcd(n, unroll)

    def step(block, carry):
        for j in range(unroll):
            body(block * unroll + j)
        return carry

    lax.fori_loop(0, n // unroll, step, 0)


def encode(packed, diag, grad):
    big = jnp.maximum(jnp.max(jnp.abs(packed), axis=0, keepdims=True), jnp.maximum(jnp.abs(diag), TINY))
    big_g = jnp.maximum(jnp.maximum(jnp.abs(grad), pltpu.roll(jnp.abs(grad), HALF, 1)), TINY)
    code = jnp.ceil(jnp.log(big) * PER)
    code_g = jnp.ceil(jnp.log(big_g) * PER)
    inv = jnp.exp2(code * (-1.0 / STEPS)) * FULL
    inv_g = jnp.exp2(code_g * (-1.0 / STEPS)) * FULL
    g = grad * inv_g
    g_hi = jnp.round(g)
    g_lo = (g - g_hi) * FULL
    first = jnp.where(iota((1, BS), 1) < HALF, diag * inv, code_g)
    return packed * inv, [first, code, g_hi, g_lo]


def put_two(coded, at, two):
    for k, (main, _) in enumerate(two):
        coded[at + (pl.ds(k * HALF, HALF),)] = to_int16(main)
    coded[at + (pl.ds(2 * HALF, 8),)] = to_int16(stack_rows(two[0][1] + two[1][1]))


def decode(main, tail):
    low = iota((1, BS), 1) < HALF
    code_g = jnp.where(low, pltpu.roll(tail[0:1], HALF, 1), tail[0:1])
    scale = jnp.exp2(tail[1:2] * (1.0 / STEPS)) * (1.0 / FULL)
    scale_g = jnp.exp2(code_g * (1.0 / STEPS)) * (1.0 / FULL)
    packed = main.astype(jnp.int32).astype(jnp.float32) * scale
    return packed, jnp.where(low, tail[0:1] * scale, 0.0), (tail[2:3] + tail[3:4] * (1.0 / FULL)) * scale_g


def get_two(coded, at):
    tail = coded[at + (pl.ds(2 * HALF, 8),)].astype(jnp.int32).astype(jnp.float32)
    return [decode(coded[at + (pl.ds(k * HALF, HALF),)], tail[4 * k : 4 * k + 4]) for k in range(2)]


def products_kernel(unroll, runs_hbm, scales_hbm, residual_hbm, jac_hbm, coded, jac, runs, scales, residual, table, sem, aux_sem):
    n_rows, groups = jac_hbm.shape[:2]
    aux = [
        pltpu.make_async_copy(runs_hbm, runs, aux_sem.at[0]),
        pltpu.make_async_copy(scales_hbm, scales, aux_sem.at[1]),
        pltpu.make_async_copy(residual_hbm, residual, aux_sem.at[2]),
    ]
    copies = [pltpu.make_async_copy(jac_hbm.at[r], jac.at[r], sem.at[r]) for r in range(n_rows)]
    for copy in aux + copies:
        copy.start()
    first = lax.axis_index("coef") * n_rows
    upper = iota((HALF, BS), 1) >= iota((HALF, BS), 0)
    lanes = iota((HALF, BS), 1) == iota((HALF, BS), 0)
    lane = iota((1, BS), 1)
    for copy in aux:
        copy.wait()
    table[...] = scales[...].astype(jnp.float32)

    def scale(half):
        run = runs[half]
        line = table[pl.ds(lax.div(run, BS), 1), :]
        return jnp.sum(jnp.where(lane == lax.rem(run, BS), line, 0.0), axis=1, keepdims=True)

    weights, terms = [], []
    for r in range(n_rows):
        row = first + r
        w = jnp.where(lane < HALF, scale(2 * row), scale(2 * row + 1))
        wr = w * residual[pl.ds(row, 1), :]
        hi = wr.astype(jnp.bfloat16).astype(jnp.float32)
        mid = (wr - hi).astype(jnp.bfloat16).astype(jnp.float32)
        split = stack_rows([hi, mid, wr - hi - mid])
        weights.append(jnp.broadcast_to(w, (BS, BS)).astype(jnp.bfloat16))
        terms.append(jnp.concatenate([split, jnp.zeros_like(split)], axis=0).astype(jnp.bfloat16))

    for r in range(n_rows):
        copies[r].wait()

        def body(g):
            two = []
            for s in range(PAIR):
                one = jac[r, g, s]
                scaled = one.T * weights[r]
                left = jnp.concatenate([scaled, terms[r]], axis=0)
                out = lax.dot_general(left, one, (((1,), (0,)), ((), ())), preferred_element_type=jnp.float32)
                last = pltpu.roll(out[HALF:BS], HALF, 1)
                packed = jnp.where(upper, out[:HALF], last)
                diag = jnp.sum(jnp.where(lanes, last, 0.0), axis=0, keepdims=True)
                grad = jnp.sum(out[BS : BS + 8], axis=0, keepdims=True)
                two.append(encode(packed, diag, grad))
            put_two(coded, (g, r), two)

        loop(groups, unroll, body)


def place_kernel(unroll, targets_hbm, coded, acc, other, targets, sem):
    copy = pltpu.make_async_copy(targets_hbm, targets, sem)
    copy.start()
    acc[...] = jnp.zeros_like(acc)
    copy.wait()

    def body(row):
        for s, (packed, diag, grad) in enumerate(get_two(coded, (row,))):
            where = targets[s, row]
            acc[where, :HALF] += packed
            acc[where, HALF:] += stack_rows([diag, grad])

    loop(coded.shape[0], unroll, body)
    theirs = 1 - lax.axis_index("core")

    def split(i):
        put_two(other, (i,), [encode_slot(acc[2 * (2 * i + k) + theirs]) for k in range(2)])

    loop(other.shape[0], unroll, split)


def encode_slot(value):
    return encode(value[:HALF], value[HALF : HALF + 1], value[HALF + 1 : HALF + 2])


def join_kernel(unroll, acc, got, coded):
    me = lax.axis_index("core")

    def body(i):
        far, bit = lax.div(i, 2), lax.rem(i, 2)
        new = ([], [])
        for k in range(2):
            at = 4 * far + 2 * k + bit
            for y, more in enumerate(get_two(got, (at,))):
                mine = acc[2 * (2 * at + y) + me]
                parts = mine[:HALF], mine[HALF : HALF + 1], mine[HALF + 1 : HALF + 2]
                new[y].append(encode(*[p + q for p, q in zip(parts, more)]))
        for y in range(2):
            put_two(coded, (2 * bit + y, far), new[y])

    loop(got.shape[0] // 2, unroll, body)


def add_up(several):
    total = several[0]
    for more in several[1:]:
        total = [x + y for x, y in zip(total, more)]
    return total


def recode_kernel(got, coded):
    for i in range(got.shape[1]):
        several = [get_two(got, (k, i)) for k in range(got.shape[0])]
        for k in range(2):
            main, tail = encode(*add_up([two[k] for two in several]))
            to = ORDER.index(2 * i + k)
            coded[to, :HALF] = to_int16(main)
            coded[to, HALF:] = to_int16(stack_rows(tail))


def finish_kernel(coded, diag_out, grad_out):
    packed, diag, grad = add_up(
        [decode(coded[k, :HALF], coded[k, HALF:].astype(jnp.int32).astype(jnp.float32)) for k in range(coded.shape[0])]
    )
    whole = jnp.concatenate([packed, pltpu.roll(packed, HALF, 1)], axis=0)
    flipped = whole.T
    r, c = iota((BS, BS), 0), iota((BS, BS), 1)
    plain = ((r < HALF) & (c >= r)) | ((c >= HALF) & (c < r))
    on = (r == c) & (r >= HALF)
    diag_out[...] = jnp.where(on, pltpu.roll(diag, HALF, 1), jnp.where(plain, whole, flipped))
    grad_out[...] = grad


def call(body, outs, specs, out="v", vmem=32, scratch=(), flops=0, moved=0):
    spaces = {"v": pltpu.VMEM, "s": pltpu.SMEM, "h": pltpu.HBM}
    spec = pl.BlockSpec(memory_space=spaces[out])
    many = isinstance(outs, (list, tuple))
    return pl.pallas_call(
        body,
        out_shape=outs,
        in_specs=[pl.BlockSpec(memory_space=spaces[k]) for k in specs],
        out_specs=[spec] * len(outs) if many else spec,
        scratch_shapes=list(scratch),
        compiler_params=pltpu.CompilerParams(vmem_limit_bytes=vmem * 1024 * 1024),
        cost_estimate=pl.CostEstimate(flops=flops, bytes_accessed=moved, transcendentals=0),
    )


def shards(jac_blocks, col_blocks, residual, run_of_half, run_scale):
    f32, i16 = jnp.float32, jnp.int16
    far = lax.axis_size("zq")
    slots = far * 8
    n_rows, groups = jac_blocks.shape[:2]
    n_items = n_rows * groups * PAIR

    def shape(n, dtype):
        return jax.ShapeDtypeStruct((n, ROWS, BS), dtype)

    targets = col_blocks[0].T
    coded = call(
        functools.partial(products_kernel, 8),
        jax.ShapeDtypeStruct((groups, n_rows, DUO, BS), i16),
        "hhhh",
        vmem=32,
        scratch=[
            pltpu.VMEM(jac_blocks.shape, jnp.bfloat16),
            pltpu.SMEM(run_of_half.shape, jnp.int32),
            pltpu.VMEM((run_scale.shape[0] // BS, BS), jnp.bfloat16),
            pltpu.VMEM(residual.shape, f32),
            pltpu.VMEM((run_scale.shape[0] // BS, BS), f32),
            pltpu.SemaphoreType.DMA((n_rows,)),
            pltpu.SemaphoreType.DMA((3,)),
        ],
        flops=2 * n_items * BS**3,
        moved=n_items * BS * BS * 3,
    )(*[pltpu.with_memory_space_constraint(x, pltpu.HBM) for x in (run_of_half, run_scale.reshape(-1, BS), residual, jac_blocks)])
    landed = lax.all_to_all(coded, "coef", 0, 0, tiled=True).reshape(n_items // PAIR, DUO, BS)
    acc, other = call(
        functools.partial(place_kernel, 16),
        [shape(slots, f32), jax.ShapeDtypeStruct((slots // 4, DUO, BS), i16)],
        "hv",
        scratch=[pltpu.SMEM(targets.shape, jnp.int32), pltpu.SemaphoreType.DMA],
    )(targets, landed)
    got = lax.ppermute(other, "core", [(0, 1), (1, 0)])
    near = slots // 2 // far
    coded = call(
        functools.partial(join_kernel, 16), jax.ShapeDtypeStruct((near, far // 2, DUO, BS), i16), "vv"
    )(acc, got)
    landed = lax.all_to_all(coded, ("z0", "yh"), 0, 0, tiled=True)
    coded = call(recode_kernel, shape(far, i16), "v")(landed)
    landed = lax.all_to_all(coded, "zq", 0, 0, tiled=True, axis_index_groups=[ORDER])
    diag, grad = call(
        finish_kernel, [jax.ShapeDtypeStruct((BS, BS), f32), jax.ShapeDtypeStruct((1, BS), f32)], "v"
    )(landed)
    return diag.reshape(1, 1, BS, BS), grad.reshape(1, 1, BS)


def solution(mesh):
    fine = Mesh(mesh.devices.reshape(-1, 2, 2, 2, mesh.devices.shape[1]), ("zq", "z0", "yh", "core", "coef"))
    batch = ("zq", "z0", "yh", "core")
    in_specs = (
        P(batch + ("coef",), None, None, None, None),
        P("coef", batch, None),
        P(batch, None),
        P(batch),
        P(),
    )
    out_specs = (P("coef", batch, None, None), P("coef", batch, None))
    return jax.shard_map(shards, mesh=fine, in_specs=in_specs, out_specs=out_specs, check_vma=False)
```

```python
import functools
import math

import jax
import jax.numpy as jnp
from jax import lax
from jax.experimental import pallas as pl
from jax.experimental.pallas import tpu as pltpu
from jax.sharding import Mesh
from jax.sharding import PartitionSpec as P

BS = 128
HALF = BS // 2
PAIR = 2
ROWS = HALF + 8
DUO = 2 * HALF + 8
FULL = 32000.0
STEPS = 16.0
TINY = 1e-30
PER = STEPS / 0.6931471805599453


ORDER = [4, 0, 6, 2, 5, 1, 7, 3]


FLIP = 7


def iota(shape, dim):
    return lax.broadcasted_iota(jnp.int32, shape, dim)


def stack_rows(rows):
    sub = iota((8, BS), 0)
    out = jnp.zeros((8, BS), jnp.float32)
    for k, row in enumerate(rows):
        out = jnp.where(sub == k, row, out)
    return out


def to_int16(x):
    return jnp.round(x).astype(jnp.int32).astype(jnp.int16)


def loop(n, unroll, body):
    unroll = math.gcd(n, unroll)

    def step(block, carry):
        for j in range(unroll):
            body(block * unroll + j)
        return carry

    lax.fori_loop(0, n // unroll, step, 0)


def encode(packed, diag, grad):
    big = jnp.maximum(jnp.max(jnp.abs(packed), axis=0, keepdims=True), jnp.maximum(jnp.abs(diag), TINY))
    big_g = jnp.maximum(jnp.maximum(jnp.abs(grad), pltpu.roll(jnp.abs(grad), HALF, 1)), TINY)
    code = jnp.ceil(jnp.log(big) * PER)
    code_g = jnp.ceil(jnp.log(big_g) * PER)
    inv = jnp.exp2(code * (-1.0 / STEPS)) * FULL
    inv_g = jnp.exp2(code_g * (-1.0 / STEPS)) * FULL
    g = grad * inv_g
    g_hi = jnp.round(g)
    g_lo = (g - g_hi) * FULL
    first = jnp.where(iota((1, BS), 1) < HALF, diag * inv, code_g)
    return packed * inv, [first, code, g_hi, g_lo]


def put_two(coded, at, two):
    for k, (main, _) in enumerate(two):
        coded[at + (pl.ds(k * HALF, HALF),)] = to_int16(main)
    coded[at + (pl.ds(2 * HALF, 8),)] = to_int16(stack_rows(two[0][1] + two[1][1]))


def decode(main, tail):
    low = iota((1, BS), 1) < HALF
    code_g = jnp.where(low, pltpu.roll(tail[0:1], HALF, 1), tail[0:1])
    scale = jnp.exp2(tail[1:2] * (1.0 / STEPS)) * (1.0 / FULL)
    scale_g = jnp.exp2(code_g * (1.0 / STEPS)) * (1.0 / FULL)
    packed = main.astype(jnp.int32).astype(jnp.float32) * scale
    return packed, jnp.where(low, tail[0:1] * scale, 0.0), (tail[2:3] + tail[3:4] * (1.0 / FULL)) * scale_g


def get_two(coded, at):
    tail = coded[at + (pl.ds(2 * HALF, 8),)].astype(jnp.int32).astype(jnp.float32)
    return [decode(coded[at + (pl.ds(k * HALF, HALF),)], tail[4 * k : 4 * k + 4]) for k in range(2)]


def products_kernel(unroll, runs_hbm, scales_hbm, residual_hbm, jac_hbm, coded, jac, runs, scales, residual, table, sem, aux_sem):
    n_rows, groups = jac_hbm.shape[:2]
    aux = [
        pltpu.make_async_copy(runs_hbm, runs, aux_sem.at[0]),
        pltpu.make_async_copy(scales_hbm, scales, aux_sem.at[1]),
        pltpu.make_async_copy(residual_hbm, residual, aux_sem.at[2]),
    ]
    copies = [pltpu.make_async_copy(jac_hbm.at[r], jac.at[r], sem.at[r]) for r in range(n_rows)]
    for copy in aux + copies:
        copy.start()
    first = lax.axis_index("coef") * n_rows
    upper = iota((HALF, BS), 1) >= iota((HALF, BS), 0)
    lanes = iota((HALF, BS), 1) == iota((HALF, BS), 0)
    lane = iota((1, BS), 1)
    for copy in aux:
        copy.wait()
    table[...] = scales[...].astype(jnp.float32)

    def scale(half):
        run = runs[half]
        line = table[pl.ds(lax.div(run, BS), 1), :]
        return jnp.sum(jnp.where(lane == lax.rem(run, BS), line, 0.0), axis=1, keepdims=True)

    weights, terms = [], []
    for r in range(n_rows):
        row = first + r
        w = jnp.where(lane < HALF, scale(2 * row), scale(2 * row + 1))
        wr = w * residual[pl.ds(row, 1), :]
        hi = wr.astype(jnp.bfloat16).astype(jnp.float32)
        mid = (wr - hi).astype(jnp.bfloat16).astype(jnp.float32)
        split = stack_rows([hi, mid, wr - hi - mid])
        weights.append(jnp.broadcast_to(w, (BS, BS)).astype(jnp.bfloat16))
        terms.append(jnp.concatenate([split, jnp.zeros_like(split)], axis=0).astype(jnp.bfloat16))

    for r in range(n_rows):
        copies[r].wait()

        def body(g):
            two = []
            for s in range(PAIR):
                one = jac[r, g, s]
                scaled = one.T * weights[r]
                left = jnp.concatenate([scaled, terms[r]], axis=0)
                out = lax.dot_general(left, one, (((1,), (0,)), ((), ())), preferred_element_type=jnp.float32)
                last = pltpu.roll(out[HALF:BS], HALF, 1)
                packed = jnp.where(upper, out[:HALF], last)
                diag = jnp.sum(jnp.where(lanes, last, 0.0), axis=0, keepdims=True)
                grad = jnp.sum(out[BS : BS + 8], axis=0, keepdims=True)
                two.append(encode(packed, diag, grad))
            put_two(coded, (lax.bitwise_xor(g, FLIP), r), two)

        loop(groups, unroll, body)


def place_kernel(unroll, targets_hbm, coded, acc, other, targets, sem):
    copy = pltpu.make_async_copy(targets_hbm, targets, sem)
    copy.start()
    acc[...] = jnp.zeros_like(acc)
    copy.wait()

    rows = coded.shape[0] // lax.axis_size("coef")

    def body(row):
        source = lax.bitwise_xor(lax.div(row, rows), FLIP)
        for s, (packed, diag, grad) in enumerate(get_two(coded, (row,))):
            where = targets[s, source * rows + lax.rem(row, rows)]
            acc[where, :HALF] += packed
            acc[where, HALF:] += stack_rows([diag, grad])

    loop(coded.shape[0], unroll, body)
    theirs = 1 - lax.axis_index("core")

    def split(i):
        put_two(other, (i,), [encode_slot(acc[2 * (2 * i + k) + theirs]) for k in range(2)])

    loop(other.shape[0], unroll, split)


def encode_slot(value):
    return encode(value[:HALF], value[HALF : HALF + 1], value[HALF + 1 : HALF + 2])


def join_kernel(unroll, acc, got, coded):
    me = lax.axis_index("core")

    def body(i):
        far, bit = lax.div(i, 2), lax.rem(i, 2)
        new = ([], [])
        for k in range(2):
            at = 4 * far + 2 * k + bit
            for y, more in enumerate(get_two(got, (at,))):
                mine = acc[2 * (2 * at + y) + me]
                parts = mine[:HALF], mine[HALF : HALF + 1], mine[HALF + 1 : HALF + 2]
                new[y].append(encode(*[p + q for p, q in zip(parts, more)]))
        for y in range(2):
            put_two(coded, (2 * bit + y, far), new[y])

    loop(got.shape[0] // 2, unroll, body)


def add_up(several):
    total = several[0]
    for more in several[1:]:
        total = [x + y for x, y in zip(total, more)]
    return total


def recode_kernel(got, coded):
    for i in range(got.shape[1]):
        several = [get_two(got, (k, i)) for k in range(got.shape[0])]
        for k in range(2):
            main, tail = encode(*add_up([two[k] for two in several]))
            to = ORDER.index(2 * i + k)
            coded[to, :HALF] = to_int16(main)
            coded[to, HALF:] = to_int16(stack_rows(tail))


def finish_kernel(coded, diag_out, grad_out):
    packed, diag, grad = add_up(
        [decode(coded[k, :HALF], coded[k, HALF:].astype(jnp.int32).astype(jnp.float32)) for k in range(coded.shape[0])]
    )
    whole = jnp.concatenate([packed, pltpu.roll(packed, HALF, 1)], axis=0)
    flipped = whole.T
    r, c = iota((BS, BS), 0), iota((BS, BS), 1)
    plain = ((r < HALF) & (c >= r)) | ((c >= HALF) & (c < r))
    on = (r == c) & (r >= HALF)
    diag_out[...] = jnp.where(on, pltpu.roll(diag, HALF, 1), jnp.where(plain, whole, flipped))
    grad_out[...] = grad


def call(body, outs, specs, out="v", vmem=32, scratch=(), flops=0, moved=0):
    spaces = {"v": pltpu.VMEM, "s": pltpu.SMEM, "h": pltpu.HBM}
    spec = pl.BlockSpec(memory_space=spaces[out])
    many = isinstance(outs, (list, tuple))
    return pl.pallas_call(
        body,
        out_shape=outs,
        in_specs=[pl.BlockSpec(memory_space=spaces[k]) for k in specs],
        out_specs=[spec] * len(outs) if many else spec,
        scratch_shapes=list(scratch),
        compiler_params=pltpu.CompilerParams(vmem_limit_bytes=vmem * 1024 * 1024),
        cost_estimate=pl.CostEstimate(flops=flops, bytes_accessed=moved, transcendentals=0),
    )


def shards(jac_blocks, col_blocks, residual, run_of_half, run_scale):
    f32, i16 = jnp.float32, jnp.int16
    far = lax.axis_size("zq")
    slots = far * 8
    n_rows, groups = jac_blocks.shape[:2]
    n_items = n_rows * groups * PAIR

    def shape(n, dtype):
        return jax.ShapeDtypeStruct((n, ROWS, BS), dtype)

    targets = col_blocks[0].T
    coded = call(
        functools.partial(products_kernel, 8),
        jax.ShapeDtypeStruct((groups, n_rows, DUO, BS), i16),
        "hhhh",
        vmem=32,
        scratch=[
            pltpu.VMEM(jac_blocks.shape, jnp.bfloat16),
            pltpu.SMEM(run_of_half.shape, jnp.int32),
            pltpu.VMEM((run_scale.shape[0] // BS, BS), jnp.bfloat16),
            pltpu.VMEM(residual.shape, f32),
            pltpu.VMEM((run_scale.shape[0] // BS, BS), f32),
            pltpu.SemaphoreType.DMA((n_rows,)),
            pltpu.SemaphoreType.DMA((3,)),
        ],
        flops=2 * n_items * BS**3,
        moved=n_items * BS * BS * 3,
    )(*[pltpu.with_memory_space_constraint(x, pltpu.HBM) for x in (run_of_half, run_scale.reshape(-1, BS), residual, jac_blocks)])
    landed = lax.all_to_all(coded, "coef", 0, 0, tiled=True, axis_index_groups=[[g ^ FLIP for g in range(groups)]]).reshape(n_items // PAIR, DUO, BS)
    acc, other = call(
        functools.partial(place_kernel, 16),
        [shape(slots, f32), jax.ShapeDtypeStruct((slots // 4, DUO, BS), i16)],
        "hv",
        scratch=[pltpu.SMEM(targets.shape, jnp.int32), pltpu.SemaphoreType.DMA],
    )(targets, landed)
    got = lax.ppermute(other, "core", [(0, 1), (1, 0)])
    near = slots // 2 // far
    coded = call(
        functools.partial(join_kernel, 16), jax.ShapeDtypeStruct((near, far // 2, DUO, BS), i16), "vv"
    )(acc, got)
    landed = lax.all_to_all(coded, ("z0", "yh"), 0, 0, tiled=True)
    coded = call(recode_kernel, shape(far, i16), "v")(landed)
    landed = lax.all_to_all(coded, "zq", 0, 0, tiled=True, axis_index_groups=[ORDER])
    diag, grad = call(
        finish_kernel, [jax.ShapeDtypeStruct((BS, BS), f32), jax.ShapeDtypeStruct((1, BS), f32)], "v"
    )(landed)
    return diag.reshape(1, 1, BS, BS), grad.reshape(1, 1, BS)


def solution(mesh):
    fine = Mesh(mesh.devices.reshape(-1, 2, 2, 2, mesh.devices.shape[1]), ("zq", "z0", "yh", "core", "coef"))
    batch = ("zq", "z0", "yh", "core")
    in_specs = (
        P(batch + ("coef",), None, None, None, None),
        P("coef", batch, None),
        P(batch, None),
        P(batch),
        P(),
    )
    out_specs = (P("coef", batch, None, None), P("coef", batch, None))
    return jax.shard_map(shards, mesh=fine, in_specs=in_specs, out_specs=out_specs, check_vma=False)
```

```python
import functools
import math

import jax
import jax.numpy as jnp
from jax import lax
from jax.experimental import pallas as pl
from jax.experimental.pallas import tpu as pltpu
from jax.sharding import Mesh
from jax.sharding import PartitionSpec as P

BS = 128
HALF = BS // 2
PAIR = 2
ROWS = HALF + 8
DUO = 2 * HALF + 8
FULL = 32000.0
STEPS = 16.0
TINY = 1e-30
PER = STEPS / 0.6931471805599453


ORDER = [4, 0, 6, 2, 5, 1, 7, 3]


FLIP = 7


def iota(shape, dim):
    return lax.broadcasted_iota(jnp.int32, shape, dim)


def stack_rows(rows):
    sub = iota((8, BS), 0)
    out = jnp.zeros((8, BS), jnp.float32)
    for k, row in enumerate(rows):
        out = jnp.where(sub == k, row, out)
    return out


def to_int16(x):
    return jnp.round(x).astype(jnp.int32).astype(jnp.int16)


def loop(n, unroll, body):
    unroll = math.gcd(n, unroll)

    def step(block, carry):
        for j in range(unroll):
            body(block * unroll + j)
        return carry

    lax.fori_loop(0, n // unroll, step, 0)


def encode(packed, diag, grad):
    big = jnp.maximum(jnp.max(jnp.abs(packed), axis=0, keepdims=True), jnp.maximum(jnp.abs(diag), TINY))
    big_g = jnp.maximum(jnp.maximum(jnp.abs(grad), pltpu.roll(jnp.abs(grad), HALF, 1)), TINY)
    code = jnp.ceil(jnp.log(big) * PER)
    code_g = jnp.ceil(jnp.log(big_g) * PER)
    inv = jnp.exp2(code * (-1.0 / STEPS)) * FULL
    inv_g = jnp.exp2(code_g * (-1.0 / STEPS)) * FULL
    g = grad * inv_g
    g_hi = jnp.round(g)
    g_lo = (g - g_hi) * FULL
    first = jnp.where(iota((1, BS), 1) < HALF, diag * inv, code_g)
    return packed * inv, [first, code, g_hi, g_lo]


def put_two(coded, at, two):
    for k, (main, _) in enumerate(two):
        coded[at + (pl.ds(k * HALF, HALF),)] = to_int16(main)
    coded[at + (pl.ds(2 * HALF, 8),)] = to_int16(stack_rows(two[0][1] + two[1][1]))


def decode(main, tail):
    low = iota((1, BS), 1) < HALF
    code_g = jnp.where(low, pltpu.roll(tail[0:1], HALF, 1), tail[0:1])
    scale = jnp.exp2(tail[1:2] * (1.0 / STEPS)) * (1.0 / FULL)
    scale_g = jnp.exp2(code_g * (1.0 / STEPS)) * (1.0 / FULL)
    packed = main.astype(jnp.int32).astype(jnp.float32) * scale
    return packed, jnp.where(low, tail[0:1] * scale, 0.0), (tail[2:3] + tail[3:4] * (1.0 / FULL)) * scale_g


def get_two(coded, at):
    tail = coded[at + (pl.ds(2 * HALF, 8),)].astype(jnp.int32).astype(jnp.float32)
    return [decode(coded[at + (pl.ds(k * HALF, HALF),)], tail[4 * k : 4 * k + 4]) for k in range(2)]


def products_kernel(unroll, runs_hbm, scales_hbm, residual_hbm, jac_hbm, coded, jac, runs, scales, residual, table, sem, aux_sem):
    n_rows, groups = jac_hbm.shape[:2]
    aux = [
        pltpu.make_async_copy(runs_hbm, runs, aux_sem.at[0]),
        pltpu.make_async_copy(scales_hbm, scales, aux_sem.at[1]),
        pltpu.make_async_copy(residual_hbm, residual, aux_sem.at[2]),
    ]
    copies = [pltpu.make_async_copy(jac_hbm.at[r], jac.at[r], sem.at[r]) for r in range(n_rows)]
    for copy in aux + copies:
        copy.start()
    first = lax.axis_index("coef") * n_rows
    upper = iota((HALF, BS), 1) >= iota((HALF, BS), 0)
    lanes = iota((HALF, BS), 1) == iota((HALF, BS), 0)
    lane = iota((1, BS), 1)
    for copy in aux:
        copy.wait()
    table[...] = scales[...].astype(jnp.float32)

    def scale(half):
        run = runs[half]
        line = table[pl.ds(lax.div(run, BS), 1), :]
        return jnp.sum(jnp.where(lane == lax.rem(run, BS), line, 0.0), axis=1, keepdims=True)

    weights, terms = [], []
    for r in range(n_rows):
        row = first + r
        w = jnp.where(lane < HALF, scale(2 * row), scale(2 * row + 1))
        wr = w * residual[pl.ds(row, 1), :]
        hi = wr.astype(jnp.bfloat16).astype(jnp.float32)
        mid = (wr - hi).astype(jnp.bfloat16).astype(jnp.float32)
        split = stack_rows([hi, mid, wr - hi - mid])
        weights.append(jnp.broadcast_to(w, (BS, BS)).astype(jnp.bfloat16))
        terms.append(jnp.concatenate([split, jnp.zeros_like(split)], axis=0).astype(jnp.bfloat16))

    for r in range(n_rows):
        copies[r].wait()

        def body(g):
            two = []
            for s in range(PAIR):
                one = jac[r, g, s]
                scaled = one.T * weights[r]
                left = jnp.concatenate([scaled, terms[r]], axis=0)
                out = lax.dot_general(left, one, (((1,), (0,)), ((), ())), preferred_element_type=jnp.float32)
                last = pltpu.roll(out[HALF:BS], HALF, 1)
                packed = jnp.where(upper, out[:HALF], last)
                diag = jnp.sum(jnp.where(lanes, last, 0.0), axis=0, keepdims=True)
                grad = jnp.sum(out[BS : BS + 8], axis=0, keepdims=True)
                two.append(encode(packed, diag, grad))
            put_two(coded, (lax.bitwise_xor(g, FLIP), r), two)

        loop(groups, unroll, body)


def place_kernel(unroll, targets_hbm, coded, acc, other, targets, sem):
    copy = pltpu.make_async_copy(targets_hbm, targets, sem)
    copy.start()
    acc[...] = jnp.zeros_like(acc)
    copy.wait()

    rows = coded.shape[0] // lax.axis_size("coef")

    def body(row):
        source = lax.bitwise_xor(lax.div(row, rows), FLIP)
        for s, (packed, diag, grad) in enumerate(get_two(coded, (row,))):
            where = targets[s, source * rows + lax.rem(row, rows)]
            acc[where, :HALF] += packed
            acc[where, HALF:] += stack_rows([diag, grad])

    loop(coded.shape[0], unroll, body)
    theirs = 1 - lax.axis_index("core")

    def split(i):
        put_two(other, (i,), [encode_slot(acc[2 * (2 * i + k) + theirs]) for k in range(2)])

    loop(other.shape[0], unroll, split)


def encode_slot(value):
    return encode(value[:HALF], value[HALF : HALF + 1], value[HALF + 1 : HALF + 2])


def join_kernel(unroll, acc, got, coded):
    me = lax.axis_index("core")

    def body(i):
        far, bit = lax.div(i, 2), lax.rem(i, 2)
        new = ([], [])
        for k in range(2):
            at = 4 * far + 2 * k + bit
            for y, more in enumerate(get_two(got, (at,))):
                mine = acc[2 * (2 * at + y) + me]
                parts = mine[:HALF], mine[HALF : HALF + 1], mine[HALF + 1 : HALF + 2]
                new[y].append(encode(*[p + q for p, q in zip(parts, more)]))
        for y in range(2):
            put_two(coded, (3 - 2 * bit - y, far), new[y])

    loop(got.shape[0] // 2, unroll, body)


def add_up(several):
    total = several[0]
    for more in several[1:]:
        total = [x + y for x, y in zip(total, more)]
    return total


def recode_kernel(got, coded):
    for i in range(got.shape[1]):
        several = [get_two(got, (k, i)) for k in range(got.shape[0])]
        for k in range(2):
            main, tail = encode(*add_up([two[k] for two in several]))
            to = ORDER.index(2 * i + k)
            coded[to, :HALF] = to_int16(main)
            coded[to, HALF:] = to_int16(stack_rows(tail))


def finish_kernel(coded, diag_out, grad_out):
    packed, diag, grad = add_up(
        [decode(coded[k, :HALF], coded[k, HALF:].astype(jnp.int32).astype(jnp.float32)) for k in range(coded.shape[0])]
    )
    whole = jnp.concatenate([packed, pltpu.roll(packed, HALF, 1)], axis=0)
    flipped = whole.T
    r, c = iota((BS, BS), 0), iota((BS, BS), 1)
    plain = ((r < HALF) & (c >= r)) | ((c >= HALF) & (c < r))
    on = (r == c) & (r >= HALF)
    diag_out[...] = jnp.where(on, pltpu.roll(diag, HALF, 1), jnp.where(plain, whole, flipped))
    grad_out[...] = grad


def call(body, outs, specs, out="v", vmem=32, scratch=(), flops=0, moved=0):
    spaces = {"v": pltpu.VMEM, "s": pltpu.SMEM, "h": pltpu.HBM}
    spec = pl.BlockSpec(memory_space=spaces[out])
    many = isinstance(outs, (list, tuple))
    return pl.pallas_call(
        body,
        out_shape=outs,
        in_specs=[pl.BlockSpec(memory_space=spaces[k]) for k in specs],
        out_specs=[spec] * len(outs) if many else spec,
        scratch_shapes=list(scratch),
        compiler_params=pltpu.CompilerParams(vmem_limit_bytes=vmem * 1024 * 1024),
        cost_estimate=pl.CostEstimate(flops=flops, bytes_accessed=moved, transcendentals=0),
    )


def shards(jac_blocks, col_blocks, residual, run_of_half, run_scale):
    f32, i16 = jnp.float32, jnp.int16
    far = lax.axis_size("zq")
    slots = far * 8
    n_rows, groups = jac_blocks.shape[:2]
    n_items = n_rows * groups * PAIR

    def shape(n, dtype):
        return jax.ShapeDtypeStruct((n, ROWS, BS), dtype)

    targets = col_blocks[0].T
    coded = call(
        functools.partial(products_kernel, 8),
        jax.ShapeDtypeStruct((groups, n_rows, DUO, BS), i16),
        "hhhh",
        vmem=32,
        scratch=[
            pltpu.VMEM(jac_blocks.shape, jnp.bfloat16),
            pltpu.SMEM(run_of_half.shape, jnp.int32),
            pltpu.VMEM((run_scale.shape[0] // BS, BS), jnp.bfloat16),
            pltpu.VMEM(residual.shape, f32),
            pltpu.VMEM((run_scale.shape[0] // BS, BS), f32),
            pltpu.SemaphoreType.DMA((n_rows,)),
            pltpu.SemaphoreType.DMA((3,)),
        ],
        flops=2 * n_items * BS**3,
        moved=n_items * BS * BS * 3,
    )(*[pltpu.with_memory_space_constraint(x, pltpu.HBM) for x in (run_of_half, run_scale.reshape(-1, BS), residual, jac_blocks)])
    landed = lax.all_to_all(coded, "coef", 0, 0, tiled=True, axis_index_groups=[[g ^ FLIP for g in range(groups)]]).reshape(n_items // PAIR, DUO, BS)
    acc, other = call(
        functools.partial(place_kernel, 16),
        [shape(slots, f32), jax.ShapeDtypeStruct((slots // 4, DUO, BS), i16)],
        "hv",
        scratch=[pltpu.SMEM(targets.shape, jnp.int32), pltpu.SemaphoreType.DMA],
    )(targets, landed)
    got = lax.ppermute(other, "core", [(0, 1), (1, 0)])
    near = slots // 2 // far
    coded = call(
        functools.partial(join_kernel, 16), jax.ShapeDtypeStruct((near, far // 2, DUO, BS), i16), "vv"
    )(acc, got)
    landed = lax.all_to_all(coded, "zy", 0, 0, tiled=True, axis_index_groups=[[i ^ 3 for i in range(4)]])
    coded = call(recode_kernel, shape(far, i16), "v")(landed)
    landed = lax.all_to_all(coded, "zq", 0, 0, tiled=True, axis_index_groups=[ORDER])
    diag, grad = call(
        finish_kernel, [jax.ShapeDtypeStruct((BS, BS), f32), jax.ShapeDtypeStruct((1, BS), f32)], "v"
    )(landed)
    return diag.reshape(1, 1, BS, BS), grad.reshape(1, 1, BS)


def solution(mesh):
    fine = Mesh(mesh.devices.reshape(-1, 4, 2, mesh.devices.shape[1]), ("zq", "zy", "core", "coef"))
    batch = ("zq", "zy", "core")
    in_specs = (
        P(batch + ("coef",), None, None, None, None),
        P("coef", batch, None),
        P(batch, None),
        P(batch),
        P(),
    )
    out_specs = (P("coef", batch, None, None), P("coef", batch, None))
    return jax.shard_map(shards, mesh=fine, in_specs=in_specs, out_specs=out_specs, check_vma=False)
```
